32 devices in a mesh: section: 8 (over z, x), tp: 4 (over y, core).
Axes of the slice: x: 2, y: 2, z: 4, core: 2. Of those that a mesh axis runs over, the one named last changes fastest.
Arguments:
- x_handed: bfloat16 [8, 768, 4096], P('section', None, 'tp'), may hold values from -6 to 6
- cot_handed: bfloat16 [8, 768, 4096], P('section', None, 'tp'), may hold values from -6 to 6
- w_query: bfloat16 [8, 4096, 4096], P('section', None, 'tp'), may hold values from -0.1875 to 0.1875
- key_value_weight: bfloat16 [8, 4096, 1024], P('section', None, 'tp'), may hold values from -0.125 to 0.125
- w_out: bfloat16 [8, 4096, 4096], P('section', 'tp'), may hold values from -0.1875 to 0.1875
- norm_gain: float32 [8, 4096], P('section'), may hold values from 0.1 to 1.9
Outputs:
- layer_out: bfloat16 [8, 768, 4096], P('section', None, 'tp')
- grad_in: bfloat16 [8, 768, 4096], P('section', None, 'tp')
- grad_query: bfloat16 [8, 4096, 4096], P('section', None, 'tp')
- grad_keyval: bfloat16 [8, 4096, 1024], P('section', None, 'tp')
- grad_out: bfloat16 [8, 4096, 4096], P('section', 'tp')
- grad_gain: float32 [8, 4096], P('section')
The draws below stay inside these ranges and needn't reach their ends.
All inputs are finite; a program needn't handle non-finite values.
Results may differ from the reference program's by a relative error of at most 0.03.
Values may be sent and summed in bfloat16 or wider, within the bound.
A program may use at most 128 MiB of HBM per device.

```python
import jax
import jax.numpy as jnp
from jax import lax

MODEL_FEATURES = 4096
HEAD_SIZE = 128
QUERY_HEADS = 32
KEY_VALUE_HEADS = 4
TOKENS = 768
RELAY_SECTIONS = 8
N_TP = 4


def block_levels(rng, dims, cuts, least, top_value):
    factor_of, own = 1.0, jax.random.fold_in(rng, 6)
    for position, parts in cuts:
        draws = jnp.exp(jax.random.uniform(jax.random.fold_in(own, position), (parts,), jnp.float32, least / len(cuts), top_value / len(cuts)))
        factor_of = factor_of * jnp.repeat(draws, dims[position] // parts).reshape([-1 if axis == position else 1 for axis in range(len(dims))])
    return factor_of


def bell_draw(stream_key, dims, spread, limit, pieces=(), kind=jnp.bfloat16):
    array = jax.random.normal(stream_key, dims, jnp.float32) * spread
    if len(pieces) > 0:
        array = block_levels(stream_key, dims, pieces, -0.22, 0.18) * array
    return jnp.clip(array, min=-limit, max=limit).astype(kind)


def setup_inputs(seed: int = 0) -> dict:
    key_of = jax.random.split(jax.random.key(seed), 7)
    return {
        "x_handed": bell_draw(key_of[0], (RELAY_SECTIONS, TOKENS, MODEL_FEATURES), 1.0, 6.0, ((0, 8), (2, 4))),
        "cot_handed": bell_draw(key_of[1], (RELAY_SECTIONS, TOKENS, MODEL_FEATURES), 1.0, 6.0, ((0, 8), (2, 4))),
        "w_query": bell_draw(key_of[2], (RELAY_SECTIONS, MODEL_FEATURES, QUERY_HEADS * HEAD_SIZE), (MODEL_FEATURES // 4) ** -0.5, 0.1875, ((0, 8), (2, 4))),
        "key_value_weight": bell_draw(key_of[3], (RELAY_SECTIONS, MODEL_FEATURES, 2 * KEY_VALUE_HEADS * HEAD_SIZE), (MODEL_FEATURES // 2) ** -0.5, 0.125, ((0, 8), (2, 4))),
        "w_out": bell_draw(key_of[4], (RELAY_SECTIONS, QUERY_HEADS * HEAD_SIZE, MODEL_FEATURES), (QUERY_HEADS * HEAD_SIZE // 4) ** -0.5, 0.1875, ((0, 8), (1, 4))),
        "norm_gain": jnp.clip(1.0 + 0.18 * jax.random.normal(key_of[5], (RELAY_SECTIONS, MODEL_FEATURES), jnp.float32), 0.1, 1.9),
    }


def round_trip(value_rows_full):
    return lax.optimization_barrier(value_rows_full.astype(jnp.bfloat16)).astype(jnp.float32)

def section_pass(operands):
    x_rows, dy_rows, w_q, w_kv, w_o, gain_row = operands
    sequence_length = x_rows.shape[0]
    heads_per_device = QUERY_HEADS // N_TP
    key_value_columns = 2 * KEY_VALUE_HEADS * HEAD_SIZE // N_TP
    query_group_width = QUERY_HEADS // KEY_VALUE_HEADS
    score_scale = HEAD_SIZE ** (-0.5)
    x_float = x_rows.astype(jnp.float32)
    inv_rms = lax.rsqrt(lax.optimization_barrier(jnp.mean(x_float * x_float, axis=-1, keepdims=True)) + 1e-05)
    unit_x = x_float * inv_rms
    normed = (unit_x * gain_row).astype(jnp.bfloat16)
    queries = jnp.dot(normed, w_q, preferred_element_type=jnp.float32).astype(jnp.bfloat16)
    key_value_pairs = jnp.dot(normed, w_kv, preferred_element_type=jnp.float32).astype(jnp.bfloat16)
    query_heads = queries.reshape(sequence_length, QUERY_HEADS, HEAD_SIZE).astype(jnp.float32)
    head_keys = jnp.repeat(key_value_pairs[:, :KEY_VALUE_HEADS * HEAD_SIZE].reshape(sequence_length, KEY_VALUE_HEADS, HEAD_SIZE), query_group_width, axis=1).astype(jnp.float32)
    head_values = jnp.repeat(key_value_pairs[:, KEY_VALUE_HEADS * HEAD_SIZE:].reshape(sequence_length, KEY_VALUE_HEADS, HEAD_SIZE), query_group_width, axis=1).astype(jnp.float32)
    scores = jnp.einsum('shd,thd->hst', query_heads, head_keys) * score_scale
    row_ids = lax.broadcasted_iota(jnp.int32, (sequence_length, sequence_length), 0)
    col_ids = lax.broadcasted_iota(jnp.int32, (sequence_length, sequence_length), 1)
    causal = row_ids >= col_ids
    scores = jnp.where(causal[None], scores, jnp.float32(-1e+30))
    row_max = lax.optimization_barrier(jnp.max(scores, axis=-1, keepdims=True))
    shifted_exp = jnp.exp(scores - row_max)
    attn_probs = shifted_exp / lax.optimization_barrier(jnp.sum(shifted_exp, axis=-1, keepdims=True))
    probs_bf = attn_probs.astype(jnp.bfloat16).astype(jnp.float32)
    attended = jnp.einsum('hst,thd->shd', probs_bf, head_values).astype(jnp.bfloat16)
    attn_flat = attended.reshape(sequence_length, QUERY_HEADS * HEAD_SIZE)
    out_terms = jnp.einsum('sgk,gkd->gsd', attn_flat.reshape(sequence_length, N_TP, heads_per_device * HEAD_SIZE).astype(jnp.float32), w_o.reshape(N_TP, heads_per_device * HEAD_SIZE, MODEL_FEATURES).astype(jnp.float32))
    mixed_rows = lax.optimization_barrier(jnp.sum(round_trip(out_terms), axis=0))
    layer_out = (x_float + mixed_rows).astype(jnp.bfloat16)
    dy_float = dy_rows.astype(jnp.float32)
    grad_out = jnp.einsum('sk,sd->kd', attn_flat.astype(jnp.float32), dy_float).astype(jnp.bfloat16)
    d_attended = jnp.einsum('sd,kd->sk', dy_float, w_o.astype(jnp.float32)).astype(jnp.bfloat16)
    d_att_heads = d_attended.reshape(sequence_length, QUERY_HEADS, HEAD_SIZE).astype(jnp.float32)
    d_probs = jnp.einsum('shd,thd->hst', d_att_heads, head_values)
    row_delta = jnp.einsum('shd,shd->hs', d_att_heads, attended.reshape(sequence_length, QUERY_HEADS, HEAD_SIZE).astype(jnp.float32))
    d_scores = (attn_probs * (d_probs - row_delta[:, :, None]) * score_scale).astype(jnp.bfloat16).astype(jnp.float32)
    d_queries = jnp.einsum('hst,thd->shd', d_scores, head_keys).astype(jnp.bfloat16).reshape(sequence_length, QUERY_HEADS * HEAD_SIZE)
    d_key_heads = jnp.einsum('hst,shd->htd', d_scores, query_heads)
    d_value_heads = jnp.einsum('hst,shd->htd', probs_bf, d_att_heads)

    def group_sum(per_head):
        share_per_device = round_trip(lax.optimization_barrier(jnp.sum(per_head.reshape(N_TP, heads_per_device, sequence_length, HEAD_SIZE), axis=1)))
        share_per_key_value = lax.optimization_barrier(jnp.sum(share_per_device.reshape(KEY_VALUE_HEADS, N_TP // KEY_VALUE_HEADS, sequence_length, HEAD_SIZE), axis=1))
        return jnp.transpose(share_per_key_value, (1, 0, 2)).reshape(sequence_length, KEY_VALUE_HEADS * HEAD_SIZE)
    d_keyvals = jnp.concatenate([group_sum(d_key_heads), group_sum(d_value_heads)], axis=1).astype(jnp.bfloat16)
    normed_float = normed.astype(jnp.float32)
    grad_query = jnp.einsum('sd,sk->dk', normed_float, d_queries.astype(jnp.float32)).astype(jnp.bfloat16)
    grad_keyval = jnp.einsum('sd,sk->dk', normed_float, d_keyvals.astype(jnp.float32)).astype(jnp.bfloat16)
    in_terms = jnp.einsum('sgk,dgk->gsd', d_queries.reshape(sequence_length, N_TP, heads_per_device * HEAD_SIZE).astype(jnp.float32), w_q.reshape(MODEL_FEATURES, N_TP, heads_per_device * HEAD_SIZE).astype(jnp.float32))
    in_terms = in_terms + jnp.einsum('sgk,dgk->gsd', d_keyvals.reshape(sequence_length, N_TP, key_value_columns).astype(jnp.float32), w_kv.reshape(MODEL_FEATURES, N_TP, key_value_columns).astype(jnp.float32))
    d_normed = lax.optimization_barrier(jnp.sum(round_trip(in_terms), axis=0))
    grad_gain = lax.optimization_barrier(jnp.sum(d_normed * unit_x, axis=0))
    d_unit = d_normed * gain_row
    d_input = inv_rms * (d_unit - unit_x * lax.optimization_barrier(jnp.mean(d_unit * unit_x, axis=-1, keepdims=True)))
    grad_in = (dy_float + d_input).astype(jnp.bfloat16)
    return (layer_out, grad_in, grad_query, grad_keyval, grad_out, grad_gain)

def reference(x_handed, cot_handed, w_query, key_value_weight, w_out, norm_gain):
    x_prev = jnp.roll(x_handed, 1, axis=0)
    dy_next = jnp.roll(cot_handed, -1, axis=0)
    results = lax.map(section_pass, (x_prev, dy_next, w_query, key_value_weight, w_out, norm_gain))
    return (results[0], results[1], results[2], results[3], results[4], results[5])
```

```python
import jax
import jax.numpy as jnp
from jax import lax
from jax.experimental import pallas as pl
from jax.experimental.pallas import tpu as pltpu
from jax.sharding import PartitionSpec as P

HEAD_SIZE = 128
QUERY_HEADS = 32
KEY_VALUE_HEADS = 4


def shifted(value, axis, steps):
    count = lax.axis_size(axis)
    pairs = [(source, (source + steps) % count) for source in range(count)]
    return lax.ppermute(value, axis, pairs)


NT = (((1,), (1,)), ((), ()))
TN = (((0,), (0,)), ((), ()))
BLOCK_ROWS = 256


def dot(left, right, dims):
    return lax.dot_general(left, right, dims, preferred_element_type=jnp.float32)


MESH = pl.DeviceIdType.MESH
CHUNK = 128
TILE = 256


def forward_kernel(
    x_ref, dy_ref, wq_hbm, wkv_hbm, wo_hbm, gain_ref,
    x_out, dy_out, normed_out, inv_ref, q_out, keyval_out, att_out, probs_out, datt_out, far_out, near_out,
    x_all, dy_all, wq, wkv, wo, normed, q, kv_part, keyval, att, probs, datt, pieces, arrived, far, near,
    load_sem, store_sem, send_sem, recv_sem, kv_send, kv_recv, piece_send, piece_recv, credit,
):
    section, me = lax.axis_index("section"), lax.axis_index("tp")
    sections = lax.axis_size("section")
    rows, width = x_ref.shape[1], x_ref.shape[2]
    parts = x_all.shape[0]
    features = parts * width
    chunks, blocks = rows // CHUNK, rows // BLOCK_ROWS
    per_block = BLOCK_ROWS // CHUNK
    heads = q.shape[1] // HEAD_SIZE
    after, before = lax.rem(section + 1, sections), lax.rem(section + sections - 1, sections)
    far_slot, near_slot, last_slot = lax.rem(me + 2, 4), me + 1 - 2 * lax.rem(me, 2), 3 - me
    across, beside = (section, far_slot), (section, near_slot)
    shift_to = ((after, me), (before, me))
    held = (x_all, dy_all)

    barrier = pltpu.get_barrier_semaphore()
    for peer in (across, beside, (section, last_slot), shift_to[0], shift_to[1]):
        pl.semaphore_signal(barrier, inc=1, device_id=peer, device_id_type=MESH)
    pl.semaphore_wait(barrier, 5)

    def span(i):
        return pl.ds(i * CHUNK, CHUNK)

    def rows_of(b):
        return pl.ds(b * BLOCK_ROWS, BLOCK_ROWS)

    def move(a, kind, i):
        slot = far_slot if kind == 3 else me
        target = held[a].at[slot, span(i)]
        source = (x_ref, dy_ref)[a].at[0, span(i)] if kind == 0 else target
        return pltpu.make_async_remote_copy(
            src_ref=source, dst_ref=target,
            send_sem=send_sem.at[a, kind, i], recv_sem=recv_sem.at[a, kind, i],
            device_id=(shift_to[a], across, beside, beside)[kind], device_id_type=MESH,
        )

    loads = {}
    for n, (name, source, target) in enumerate(
        (("kv", wkv_hbm, wkv), ("q", wq_hbm, wq), ("o", wo_hbm, wo))
    ):
        loads[name] = pltpu.make_async_copy(source.at[0], target, load_sem.at[n])

    stores = []

    def store(source, target):
        copy = pltpu.make_async_copy(source, target, store_sem.at[len(stores)])
        copy.start()
        stores.append(copy)

    for i in range(chunks):
        move(0, 0, i).start()
    for name in ("kv", "q", "o"):
        loads[name].start()

    def relay(a, i):
        if i < chunks:
            move(a, 0, i).wait_recv()
            move(a, 1, i).start()
            move(a, 2, i).start()
        if i > 0:
            move(a, 1, i - 1).wait_recv()
            move(a, 3, i - 1).start()

    def gathered(a, i):
        move(a, 2, i).wait_recv()
        move(a, 3, i).wait_recv()

    def normalise(i):
        gathered(0, i)
        step = 32

        @pl.loop(0, CHUNK // step)
        def _(r):
            here = pl.ds(pl.multiple_of(i * CHUNK + r * step, step), step)
            local = pl.ds(pl.multiple_of((i % per_block) * CHUNK + r * step, step), step)
            total = jnp.zeros((step, 1), jnp.float32)
            for p in range(parts):
                value = x_all[p, here].astype(jnp.float32)
                total += jnp.sum(value * value, axis=-1, keepdims=True)
            inv = lax.rsqrt(total / features + 1e-05)
            inv_ref[here, :] = jnp.broadcast_to(inv, (step, inv_ref.shape[1]))
            for p in range(parts):
                value = x_all[p, here].astype(jnp.float32)
                cols = slice(p * width, (p + 1) * width)
                normed[(i // per_block) % 2, local, cols] = (value * inv * gain_ref[0:1, cols]).astype(jnp.bfloat16)

    def kv_copy(b, half):
        owner = 2 * lax.rem(me, 2) + half
        return owner, pltpu.make_async_remote_copy(
            src_ref=kv_part.at[half, rows_of(b)], dst_ref=keyval.at[me // 2, rows_of(b)],
            send_sem=kv_send.at[half, b], recv_sem=kv_recv.at[me // 2, b],
            device_id=(section, owner), device_id_type=MESH,
        )

    def project(b):
        here = rows_of(b)
        store(normed.at[b % 2], normed_out.at[here])
        if b == 0:
            loads["kv"].wait()
        pair = jnp.dot(normed[b % 2], wkv[...], preferred_element_type=jnp.float32).astype(jnp.bfloat16)
        for half in range(2):
            kv_part[half, here, :] = pair[:, half * HEAD_SIZE:(half + 1) * HEAD_SIZE]
        for half in range(2):
            owner, copy = kv_copy(b, half)

            @pl.when(owner != me)
            def _():
                copy.start()

            @pl.when(owner == me)
            def _():
                keyval[me // 2, here, :] = kv_part[half, here, :]
        if b == 0:
            loads["q"].wait()

        @pl.loop(0, q.shape[1] // TILE)
        def _(n):
            cols = pl.ds(pl.multiple_of(n * TILE, TILE), TILE)
            q[here, cols] = jnp.dot(
                normed[b % 2], wq[:, cols], preferred_element_type=jnp.float32
            ).astype(jnp.bfloat16)

    def receive_kv(b):
        for kind, own in ((0, 0), (1, 3)):

            @pl.when(me != own)
            def _():
                pltpu.make_async_remote_copy(
                    src_ref=kv_part.at[0, rows_of(b)], dst_ref=keyval.at[kind, rows_of(b)],
                    send_sem=kv_send.at[0, b], recv_sem=kv_recv.at[kind, b],
                    device_id=beside, device_id_type=MESH,
                ).wait_recv()

    def attention(b, first, last):
        start, stop = b * BLOCK_ROWS, (b + 1) * BLOCK_ROWS
        here = slice(start, stop)

        @pl.loop(first, last)
        def _(h):
            cols = pl.ds(pl.multiple_of(h * HEAD_SIZE, HEAD_SIZE), HEAD_SIZE)
            scores = dot(q[here, cols], keyval[0, :stop, :], NT) * (HEAD_SIZE ** (-0.5))
            row_ids = lax.broadcasted_iota(jnp.int32, scores.shape, 0) + start
            col_ids = lax.broadcasted_iota(jnp.int32, scores.shape, 1)
            scores = jnp.where(row_ids >= col_ids, scores, jnp.float32(-1e30))
            top = jnp.max(scores, axis=-1, keepdims=True)
            powers = jnp.exp(scores - top)
            share = powers * (1.0 / jnp.sum(powers, axis=-1, keepdims=True))
            share = share.astype(jnp.bfloat16)
            probs[h, :, :stop] = share
            att[here, cols] = jnp.dot(
                share, keyval[1, :stop, :], preferred_element_type=jnp.float32
            ).astype(jnp.bfloat16)

    def attention_done(b):
        start, stop = b * BLOCK_ROWS, (b + 1) * BLOCK_ROWS
        store(probs.at[:, :, :stop], probs_out.at[:, start:stop, :stop])
        return len(stores) - 1

    def piece_copy(b, n):
        return pltpu.make_async_remote_copy(
            src_ref=pieces.at[n, rows_of(b)], dst_ref=arrived.at[n, rows_of(b)],
            send_sem=piece_send.at[n, b], recv_sem=piece_recv.at[n, b],
            device_id=beside, device_id_type=MESH,
        )

    def mix(b):
        here = rows_of(b)
        if b == 0:
            loads["o"].wait()

        def term(owner, tile):
            cols = pl.ds(pl.multiple_of(owner * width + tile * TILE, TILE), TILE)
            return jnp.dot(att[here, :], wo[:, cols], preferred_element_type=jnp.float32)

        for n, owner in ((0, last_slot), (1, near_slot)):

            @pl.loop(0, width // TILE)
            def _(tile):
                cols = pl.ds(pl.multiple_of(tile * TILE, TILE), TILE)
                pieces[n, here, cols] = term(owner, tile).astype(jnp.bfloat16)

            piece_copy(b, n).start()
        piece_copy(b, 0).wait_recv()

        @pl.loop(0, width // TILE)
        def _(tile):
            cols = pl.ds(pl.multiple_of(tile * TILE, TILE), TILE)
            value = term(far_slot, tile) + arrived[0, here, cols].astype(jnp.float32)
            far[here, cols] = value.astype(jnp.bfloat16)

        store(far.at[here], far_out.at[here])
        piece_copy(b, 1).wait_recv()

        @pl.loop(0, width // TILE)
        def _(tile):
            cols = pl.ds(pl.multiple_of(tile * TILE, TILE), TILE)
            value = term(me, tile) + arrived[1, here, cols].astype(jnp.float32)
            near[here, cols] = value + x_all[me, here, cols].astype(jnp.float32)

        store(near.at[here], near_out.at[here])

    def backward_in(b):
        here = rows_of(b)
        for i in range(b * per_block, (b + 1) * per_block):
            gathered(1, i)
        for p in range(parts):
            store(dy_all.at[p, here], dy_out.at[here, pl.ds(p * width, width)])

        @pl.loop(0, datt.shape[1] // TILE)
        def _(n):
            some = pl.ds(pl.multiple_of(n * TILE, TILE), TILE)
            value = jnp.zeros((BLOCK_ROWS, TILE), jnp.float32)
            for p in range(parts):
                value += dot(dy_all[p, here, :], wo[some, p * width:(p + 1) * width], NT)
            datt[here, some] = value.astype(jnp.bfloat16)

    relay(0, 0)
    relay(0, 1)
    relay(0, 2)
    normalise(0)
    relay(0, 3)
    normalise(1)
    project(0)
    relay(0, 4)
    normalise(2)
    receive_kv(0)
    attention(0, 0, heads)
    held_probs = attention_done(0)
    relay(0, 5)
    pl.semaphore_signal(credit, inc=1, device_id=(after, me), device_id_type=MESH)
    normalise(3)
    pl.semaphore_wait(credit, 1)
    for i in range(chunks):
        move(1, 0, i).start()
    project(1)
    relay(0, 6)
    stores[0].wait()
    normalise(4)
    receive_kv(1)
    relay(1, 0)
    stores[held_probs].wait()
    attention(1, 0, heads)
    later_probs = attention_done(1)
    normalise(5)
    relay(1, 1)
    store(x_all.at[me], x_out)
    project(2)
    receive_kv(2)
    store(keyval, keyval_out)
    store(q, q_out)
    relay(1, 2)
    stores[later_probs].wait()
    attention(2, 0, heads // 2)
    relay(1, 3)
    attention(2, heads // 2, heads)
    attention_done(2)
    store(att, att_out)
    relay(1, 4)
    mix(0)
    backward_in(0)
    relay(1, 5)
    mix(1)
    backward_in(1)
    relay(1, 6)
    mix(2)
    backward_in(2)
    store(datt, datt_out)

    for a in range(2):
        for kind in range(4):
            for i in range(chunks):
                move(a, kind, i).wait_send()
    for b in range(blocks):
        for half in range(2):
            owner, copy = kv_copy(b, half)

            @pl.when(owner != me)
            def _():
                copy.wait_send()
        for n in range(2):
            piece_copy(b, n).wait_send()
    for n, copy in enumerate(stores):
        if n not in (0, held_probs, later_probs):
            copy.wait()


def forward(x_handed, cot_handed, w_query, key_value_weight, w_out, norm_gain):
    rows, width = x_handed.shape[1:]
    features, heads = w_query.shape[1], w_query.shape[2] // HEAD_SIZE
    inner = heads * HEAD_SIZE
    chunks, blocks = rows // CHUNK, rows // BLOCK_ROWS
    parts = features // width
    bf16, f32 = jnp.bfloat16, jnp.float32
    anywhere = pl.BlockSpec(memory_space=pl.ANY)
    local = pl.BlockSpec(memory_space=pltpu.VMEM)
    dma = pltpu.SemaphoreType.DMA
    kv_rows = (2, rows, HEAD_SIZE)
    shapes = [
        ((rows, width), bf16), ((rows, features), bf16), ((rows, features), bf16), ((rows, 128), f32),
        ((rows, inner), bf16), (kv_rows, bf16), ((rows, inner), bf16), ((heads, rows, rows), bf16),
        ((rows, inner), bf16), ((rows, width), bf16), ((rows, width), f32),
    ]
    return pl.pallas_call(
        forward_kernel,
        out_shape=[jax.ShapeDtypeStruct(*s) for s in shapes],
        in_specs=[anywhere] * 5 + [local],
        out_specs=[local if n == 3 else anywhere for n in range(len(shapes))],
        scratch_shapes=[
            pltpu.VMEM((parts, rows, width), bf16),
            pltpu.VMEM((parts, rows, width), bf16),
            pltpu.VMEM(w_query.shape[1:], bf16),
            pltpu.VMEM(key_value_weight.shape[1:], bf16),
            pltpu.VMEM(w_out.shape[1:], bf16),
            pltpu.VMEM((2, BLOCK_ROWS, features), bf16),
            pltpu.VMEM((rows, inner), bf16),
            pltpu.VMEM(kv_rows, bf16),
            pltpu.VMEM(kv_rows, bf16),
            pltpu.VMEM((rows, inner), bf16),
            pltpu.VMEM((heads, BLOCK_ROWS, rows), bf16),
            pltpu.VMEM((rows, inner), bf16),
            pltpu.VMEM((2, rows, width), bf16),
            pltpu.VMEM((2, rows, width), bf16),
            pltpu.VMEM((rows, width), bf16),
            pltpu.VMEM((rows, width), f32),
            dma((3,)),
            dma((40,)),
            dma((2, 4, chunks)),
            dma((2, 4, chunks)),
            dma((2, blocks)),
            dma((2, blocks)),
            dma((2, blocks)),
            dma((2, blocks)),
            pltpu.SemaphoreType.REGULAR,
        ],
        compiler_params=pltpu.CompilerParams(
            collective_id=0, has_side_effects=True, vmem_limit_bytes=60 << 20
        ),
        cost_estimate=pl.CostEstimate(
            flops=8 * rows * features * inner, bytes_accessed=60 << 20, transcendentals=heads * rows * rows
        ),
    )(x_handed, cot_handed, w_query, key_value_weight, w_out, norm_gain)


def backward_kernel(q_ref, k_ref, v_ref, out_ref, dout_ref, probs_ref, dq_ref, dk_ref, dv_ref):
    rows = q_ref.shape[0]

    @pl.when(pl.program_id(0) == 0)
    def _():
        dk_ref[...] = jnp.zeros_like(dk_ref)
        dv_ref[...] = jnp.zeros_like(dv_ref)

    for start in range(0, rows, BLOCK_ROWS):
        stop = start + BLOCK_ROWS
        here = slice(start, stop)
        d_out = dout_ref[here, :]
        delta = jnp.sum(
            d_out.astype(jnp.float32) * out_ref[here, :].astype(jnp.float32), axis=-1, keepdims=True
        )
        probs = probs_ref[0, here, :stop]
        d_probs = dot(d_out, v_ref[:stop, :], NT)
        d_scores = probs.astype(jnp.float32) * (d_probs - delta) * (HEAD_SIZE ** (-0.5))
        d_scores = d_scores.astype(jnp.bfloat16)
        dq_ref[here, :] = jnp.dot(
            d_scores, k_ref[:stop, :], preferred_element_type=jnp.float32
        ).astype(jnp.bfloat16)
        dk_ref[:stop, :] += dot(d_scores, q_ref[here, :], TN)
        dv_ref[:stop, :] += dot(probs, d_out, TN)


def attend_backward(queries, keys, values, attended, d_attended, probs):
    rows = queries.shape[0]
    heads = queries.shape[1] // HEAD_SIZE
    column = pl.BlockSpec((rows, HEAD_SIZE), lambda h: (0, h))
    fixed = pl.BlockSpec((rows, HEAD_SIZE), lambda h: (0, 0))
    return pl.pallas_call(
        backward_kernel,
        grid=(heads,),
        in_specs=[column, fixed, fixed, column, column,
                  pl.BlockSpec((1, rows, rows), lambda h: (h, 0, 0))],
        out_specs=[column, fixed, fixed],
        out_shape=[
            jax.ShapeDtypeStruct(queries.shape, jnp.bfloat16),
            jax.ShapeDtypeStruct(keys.shape, jnp.float32),
            jax.ShapeDtypeStruct(keys.shape, jnp.float32),
        ],
        compiler_params=pltpu.CompilerParams(vmem_limit_bytes=40 << 20),
        cost_estimate=pl.CostEstimate(
            flops=20 * heads * rows * rows * HEAD_SIZE,
            bytes_accessed=2 * heads * rows * (rows + 4 * HEAD_SIZE),
            transcendentals=0,
        ),
    )(queries, keys, values, attended, d_attended, probs)


def scattered(term, width, operands):
    me = lax.axis_index("tp")
    count = lax.axis_size("tp")
    core_pairs = [(i, i ^ 1) for i in range(count)]
    far_pairs = [(i, i ^ 2) for i in range(count)]
    core, row = me % 2, me // 2
    far, near = 1 - row, row

    def block(r, c):
        return term((2 * r + c) * width, *operands)

    far_other = block(far, 1 - core).astype(jnp.bfloat16)
    far_arrived = lax.ppermute(far_other, "tp", core_pairs)
    far_mine = block(far, core)
    far_sum = (far_mine + far_arrived.astype(jnp.float32)).astype(jnp.bfloat16)
    far_sum, operands = lax.optimization_barrier((far_sum, operands))
    across = lax.ppermute(far_sum, "tp", far_pairs)
    near_other = block(near, 1 - core).astype(jnp.bfloat16)
    near_arrived = lax.ppermute(near_other, "tp", core_pairs)
    near_mine = block(near, core)
    return near_mine + near_arrived.astype(jnp.float32), across, operands


def on_device(x_handed, cot_handed, w_query, key_value_weight, w_out, norm_gain):
    wq_dev = w_query[0]
    wkv_dev = key_value_weight[0]
    gain_row = norm_gain[0]
    features = wq_dev.shape[0]
    me = lax.axis_index("tp")
    (
        x_part, dy_all, normed_all, inv_rms, queries, keyval, attended, probs, d_attended, mixed_out, mixed_near
    ) = forward(x_handed, cot_handed, w_query, key_value_weight, w_out, norm_gain)
    keys, values = keyval[0], keyval[1]
    inv_rms = inv_rms[:, :1]
    width = x_part.shape[1]
    mine = me * width
    dy_part = lax.dynamic_slice_in_dim(dy_all, mine, width, 1)
    far_pairs = [(i, i ^ 2) for i in range(lax.axis_size("tp"))]
    mixed_far = lax.ppermute(mixed_out, "tp", far_pairs)
    layer_out = (mixed_near + mixed_far.astype(jnp.float32)).astype(jnp.bfloat16)
    d_queries, d_keys, d_values = attend_backward(
        queries, keys, values, attended, d_attended, probs
    )
    pair = jnp.concatenate([d_keys, d_values], axis=1).astype(jnp.bfloat16)
    pairs = lax.all_gather(pair, "tp", axis=1, tiled=True)
    kv_width = wkv_dev.shape[1]
    half = KEY_VALUE_HEADS // 2
    first_kv = 2 * HEAD_SIZE * half * (me % 2) + HEAD_SIZE * (me // 2)
    d_kv_mine = jnp.concatenate(
        [
            lax.dynamic_slice_in_dim(pairs, first_kv + 2 * HEAD_SIZE * g, HEAD_SIZE, 1)
            for g in range(half)
        ],
        axis=1,
    )
    grad_query = dot(normed_all, d_queries, TN).astype(jnp.bfloat16)
    d_kv_mine, d_queries, grad_query = lax.optimization_barrier((d_kv_mine, d_queries, grad_query))

    def in_term(first, d_queries, d_kv_mine, *later):
        block = lax.dynamic_slice_in_dim(wq_dev, first, width, 0)
        kv_block = lax.dynamic_slice_in_dim(wkv_dev, first, width, 0)
        return dot(d_queries, block, NT) + dot(d_kv_mine, kv_block, NT)

    d_near, d_far, (d_queries, d_kv_mine, attended, normed_all) = scattered(
        in_term, width, (d_queries, d_kv_mine, attended, normed_all)
    )
    grad_out = dot(attended, dy_all, TN).astype(jnp.bfloat16)
    grad_keyval = dot(normed_all, d_kv_mine, TN).astype(jnp.bfloat16)

    def product(a, b):
        return jnp.sum(a.astype(jnp.float32) * b.astype(jnp.float32), axis=1)

    row_dot = product(d_queries, queries) + product(
        pair, jnp.concatenate([keys, values], axis=1)
    )
    row_dot = jnp.sum(lax.all_gather(row_dot, "tp"), axis=0)
    row_mean = (row_dot / features)[:, None]
    gain_mine = lax.dynamic_slice_in_dim(gain_row, mine, width, 0)
    unit_mine = x_part.astype(jnp.float32) * inv_rms
    d_normed = d_near + d_far.astype(jnp.float32)
    grad_gain = lax.all_gather(jnp.sum(d_normed * unit_mine, axis=0), "tp", tiled=True)
    d_unit = d_normed * gain_mine
    grad_in = (
        dy_part.astype(jnp.float32) + inv_rms * (d_unit - unit_mine * row_mean)
    ).astype(jnp.bfloat16)
    return (
        layer_out[None],
        grad_in[None],
        grad_query[None],
        grad_keyval[None],
        grad_out[None],
        grad_gain[None],
    )


def on_device_any(x_handed, cot_handed, w_query, key_value_weight, w_out, norm_gain):
    x_part = shifted(x_handed, "section", 1)[0]
    dy_part = shifted(cot_handed, "section", -1)[0]
    wq_dev = w_query[0]
    wkv_dev = key_value_weight[0]
    wo_dev = w_out[0]
    gain_row = norm_gain[0]
    heads_per_device = wq_dev.shape[1] // HEAD_SIZE
    score_scale = HEAD_SIZE ** (-0.5)
    x_all = lax.all_gather(x_part, "tp", axis=1, tiled=True)
    sequence_length = x_all.shape[0]
    tok_rows = sequence_length // lax.axis_size("tp")
    row_start = lax.axis_index("tp") * tok_rows
    x_float = x_all.astype(jnp.float32)
    inv_rms = lax.rsqrt(jnp.mean(x_float * x_float, axis=-1, keepdims=True) + 1e-05)
    unit_x = x_float * inv_rms
    normed_all = (unit_x * gain_row).astype(jnp.bfloat16)
    queries = jnp.dot(normed_all, wq_dev, preferred_element_type=jnp.float32).astype(jnp.bfloat16)
    kv_part = jnp.dot(normed_all, wkv_dev, preferred_element_type=jnp.float32).astype(jnp.bfloat16)
    key_value_pairs = lax.all_gather(kv_part, "tp", axis=1, tiled=True)
    key_value_head = lax.axis_index("tp") * heads_per_device // (QUERY_HEADS // KEY_VALUE_HEADS)
    key_rows = lax.dynamic_slice_in_dim(key_value_pairs, key_value_head * HEAD_SIZE, HEAD_SIZE, 1)
    value_rows_full = lax.dynamic_slice_in_dim(
        key_value_pairs, KEY_VALUE_HEADS * HEAD_SIZE + key_value_head * HEAD_SIZE, HEAD_SIZE, 1
    )
    query_heads = queries.reshape(sequence_length, heads_per_device, HEAD_SIZE)
    scores = (
        jnp.einsum("shd,td->hst", query_heads, key_rows, preferred_element_type=jnp.float32)
        * score_scale
    )
    row_ids = lax.broadcasted_iota(jnp.int32, (sequence_length, sequence_length), 0)
    col_ids = lax.broadcasted_iota(jnp.int32, (sequence_length, sequence_length), 1)
    causal = row_ids >= col_ids
    scores = jnp.where(causal[None], scores, jnp.float32(-1e30))
    row_max = jnp.max(scores, axis=-1, keepdims=True)
    shifted_exp = jnp.exp(scores - row_max)
    attn_probs = shifted_exp / jnp.sum(shifted_exp, axis=-1, keepdims=True)
    probs_bf = attn_probs.astype(jnp.bfloat16)
    attended = jnp.einsum(
        "hst,td->shd", probs_bf, value_rows_full, preferred_element_type=jnp.float32
    ).astype(jnp.bfloat16)
    attn_flat = attended.reshape(sequence_length, heads_per_device * HEAD_SIZE)
    out_terms = jnp.dot(attn_flat, wo_dev, preferred_element_type=jnp.float32)
    mixed_part = lax.psum_scatter(
        out_terms.astype(jnp.bfloat16), "tp", scatter_dimension=1, tiled=True
    ).astype(jnp.float32)
    layer_out = (x_part.astype(jnp.float32) + mixed_part).astype(jnp.bfloat16)
    dy_all = lax.all_gather(dy_part, "tp", axis=1, tiled=True)
    grad_out = jnp.einsum(
        "sk,sd->kd", attn_flat, dy_all, preferred_element_type=jnp.float32
    ).astype(jnp.bfloat16)
    d_attended = jnp.einsum("sd,kd->sk", dy_all, wo_dev, preferred_element_type=jnp.float32).astype(
        jnp.bfloat16
    )
    d_att_heads = d_attended.reshape(sequence_length, heads_per_device, HEAD_SIZE)
    d_probs = jnp.einsum(
        "shd,td->hst", d_att_heads, value_rows_full, preferred_element_type=jnp.float32
    )
    row_delta = jnp.einsum(
        "shd,shd->hs", d_att_heads.astype(jnp.float32), attended.astype(jnp.float32)
    )
    d_scores = (attn_probs * (d_probs - row_delta[:, :, None]) * score_scale).astype(jnp.bfloat16)
    d_queries = jnp.einsum("hst,td->shd", d_scores, key_rows, preferred_element_type=jnp.float32)
    d_queries = d_queries.astype(jnp.bfloat16).reshape(
        sequence_length, heads_per_device * HEAD_SIZE
    )
    d_key_rows = jnp.einsum(
        "hst,shd->td", d_scores, query_heads, preferred_element_type=jnp.float32
    )
    value_row_gradient = jnp.einsum(
        "hst,shd->td", probs_bf, d_att_heads, preferred_element_type=jnp.float32
    )
    key_value_contribution = jnp.zeros(
        (sequence_length, 2 * KEY_VALUE_HEADS * HEAD_SIZE), jnp.float32
    )
    key_value_contribution = lax.dynamic_update_slice(
        key_value_contribution, d_key_rows, (jnp.int32(0), key_value_head * HEAD_SIZE)
    )
    key_value_contribution = lax.dynamic_update_slice(
        key_value_contribution,
        value_row_gradient,
        (jnp.int32(0), KEY_VALUE_HEADS * HEAD_SIZE + key_value_head * HEAD_SIZE),
    )
    d_keyvals = lax.psum_scatter(
        key_value_contribution.astype(jnp.bfloat16), "tp", scatter_dimension=1, tiled=True
    )
    grad_query = jnp.einsum(
        "sd,sk->dk", normed_all, d_queries, preferred_element_type=jnp.float32
    ).astype(jnp.bfloat16)
    grad_keyval = jnp.einsum(
        "sd,sk->dk", normed_all, d_keyvals, preferred_element_type=jnp.float32
    ).astype(jnp.bfloat16)
    from_query = jnp.einsum("sk,dk->sd", d_queries, wq_dev, preferred_element_type=jnp.float32)
    from_keyval = jnp.einsum("sk,dk->sd", d_keyvals, wkv_dev, preferred_element_type=jnp.float32)
    d_normed = lax.psum_scatter(
        (from_query + from_keyval).astype(jnp.bfloat16), "tp", scatter_dimension=0, tiled=True
    ).astype(jnp.float32)
    unit_rows = lax.dynamic_slice_in_dim(unit_x, row_start, tok_rows, 0)
    inv_rows = lax.dynamic_slice_in_dim(inv_rms, row_start, tok_rows, 0)
    dy_rows = lax.dynamic_slice_in_dim(dy_all, row_start, tok_rows, 0).astype(jnp.float32)
    gain_local = jnp.sum(d_normed * unit_rows, axis=0)
    grad_gain = lax.psum(gain_local, "tp")
    d_unit = d_normed * gain_row
    d_input = inv_rows * (d_unit - unit_rows * jnp.mean(d_unit * unit_rows, axis=-1, keepdims=True))
    grad_rows = (dy_rows + d_input).astype(jnp.bfloat16)
    grad_in = lax.all_to_all(grad_rows, "tp", split_axis=1, concat_axis=0, tiled=True)
    return (
        layer_out[None],
        grad_in[None],
        grad_query[None],
        grad_keyval[None],
        grad_out[None],
        grad_gain[None],
    )


def solution(mesh):
    return jax.shard_map(
        on_device if mesh.shape["tp"] == KEY_VALUE_HEADS else on_device_any,
        mesh=mesh,
        in_specs=(
            P("section", None, "tp"),
            P("section", None, "tp"),
            P("section", None, "tp"),
            P("section", None, "tp"),
            P("section", "tp", None),
            P("section", None),
        ),
        out_specs=(
            P("section", None, "tp"),
            P("section", None, "tp"),
            P("section", None, "tp"),
            P("section", None, "tp"),
            P("section", "tp", None),
            P("section", None),
        ),
        check_vma=False,
    )
```

```python
import jax
import jax.numpy as jnp
from jax import lax
from jax.experimental import pallas as pl
from jax.experimental.pallas import tpu as pltpu
from jax.sharding import PartitionSpec as P

HEAD_SIZE = 128
QUERY_HEADS = 32
KEY_VALUE_HEADS = 4


def shifted(value, axis, steps):
    count = lax.axis_size(axis)
    pairs = [(source, (source + steps) % count) for source in range(count)]
    return lax.ppermute(value, axis, pairs)


NT = (((1,), (1,)), ((), ()))
TN = (((0,), (0,)), ((), ()))
BLOCK_ROWS = 256


def dot(left, right, dims):
    return lax.dot_general(left, right, dims, preferred_element_type=jnp.float32)


MESH = pl.DeviceIdType.MESH
CHUNK = 128
TILE = 256


def layer_kernel(
    x_ref, dy_ref, wq_hbm, wkv_hbm, wo_hbm, gain_ref,
    x_out, dy_out, normed_out, inv_ref, att_out, mixed_out, near_out, dq_out, dkv_out, d_far_out, d_near_out, dot_ref,
    x_all, dy_all, wq, wkv, wo, normed, q, kv_part, keyval, att, probs_0, probs_1, probs_2, datt,
    pieces, arrived, far, near, dq, dk, dv, pair, dkv, dots,
    load_sem, store_sem, send_sem, recv_sem, kv_send, kv_recv, piece_send, piece_recv, far_send, far_recv,
    dkv_send, dkv_recv, d_send, d_recv, dot_send, dot_recv, credit,
):
    section, me = lax.axis_index("section"), lax.axis_index("tp")
    sections = lax.axis_size("section")
    rows, width = x_ref.shape[1], x_ref.shape[2]
    parts = x_all.shape[0]
    features = parts * width
    chunks, blocks = rows // CHUNK, rows // BLOCK_ROWS
    per_block = BLOCK_ROWS // CHUNK
    heads = q.shape[1] // HEAD_SIZE
    after, before = lax.rem(section + 1, sections), lax.rem(section + sections - 1, sections)
    far_slot, near_slot, last_slot = lax.rem(me + 2, 4), me + 1 - 2 * lax.rem(me, 2), 3 - me
    across, beside = (section, far_slot), (section, near_slot)
    shift_to = ((after, me), (before, me))
    held = (x_all, dy_all)
    probs = (probs_0, probs_1, probs_2)

    barrier = pltpu.get_barrier_semaphore()
    for peer in (across, beside, (section, last_slot), shift_to[0], shift_to[1]):
        pl.semaphore_signal(barrier, inc=1, device_id=peer, device_id_type=MESH)
    pl.semaphore_wait(barrier, 5)

    def span(i):
        return pl.ds(i * CHUNK, CHUNK)

    def rows_of(b):
        return pl.ds(b * BLOCK_ROWS, BLOCK_ROWS)

    def move(a, kind, i):
        slot = far_slot if kind == 3 else me
        target = held[a].at[slot, span(i)]
        source = (x_ref, dy_ref)[a].at[0, span(i)] if kind == 0 else target
        return pltpu.make_async_remote_copy(
            src_ref=source, dst_ref=target,
            send_sem=send_sem.at[a, kind, i], recv_sem=recv_sem.at[a, kind, i],
            device_id=(shift_to[a], across, beside, beside)[kind], device_id_type=MESH,
        )

    loads = {}
    for n, (name, source, target) in enumerate(
        (("kv", wkv_hbm, wkv), ("q", wq_hbm, wq), ("o", wo_hbm, wo))
    ):
        loads[name] = pltpu.make_async_copy(source.at[0], target, load_sem.at[n])

    stores = []

    def store(source, target):
        copy = pltpu.make_async_copy(source, target, store_sem.at[len(stores)])
        copy.start()
        stores.append(copy)
        return len(stores) - 1

    waited = set()

    def stored(*tokens):
        for n in tokens:
            stores[n].wait()
            waited.add(n)

    for i in range(chunks):
        move(0, 0, i).start()
    for name in ("kv", "q", "o"):
        loads[name].start()

    def relay(a, i):
        if i < chunks:
            move(a, 0, i).wait_recv()
            if a == 0 and i == chunks - 1:
                pl.semaphore_signal(credit, inc=1, device_id=shift_to[0], device_id_type=MESH)
            move(a, 1, i).start()
            move(a, 2, i).start()
            if a == 0 and i == chunks - 1:
                pl.semaphore_wait(credit, 1)
                for j in range(chunks):
                    move(1, 0, j).start()
        if i > 0:
            move(a, 1, i - 1).wait_recv()
            move(a, 3, i - 1).start()

    def gathered(a, i):
        move(a, 2, i).wait_recv()
        move(a, 3, i).wait_recv()

    def normalise(i):
        gathered(0, i)
        step = 32

        @pl.loop(0, CHUNK // step)
        def _(r):
            here = pl.ds(pl.multiple_of(i * CHUNK + r * step, step), step)
            local = pl.ds(pl.multiple_of((i % per_block) * CHUNK + r * step, step), step)
            total = jnp.zeros((step, 1), jnp.float32)
            for p in range(parts):
                value = x_all[p, here].astype(jnp.float32)
                total += jnp.sum(value * value, axis=-1, keepdims=True)
            inv = lax.rsqrt(total / features + 1e-05)
            inv_ref[here, :] = jnp.broadcast_to(inv, (step, inv_ref.shape[1]))
            for p in range(parts):
                value = x_all[p, here].astype(jnp.float32)
                cols = slice(p * width, (p + 1) * width)
                normed[local, cols] = (value * inv * gain_ref[0:1, cols]).astype(jnp.bfloat16)

    def kv_copy(b, half):
        owner = 2 * lax.rem(me, 2) + half
        return owner, pltpu.make_async_remote_copy(
            src_ref=kv_part.at[half, rows_of(b)], dst_ref=keyval.at[me // 2, rows_of(b)],
            send_sem=kv_send.at[half, b], recv_sem=kv_recv.at[me // 2, b],
            device_id=(section, owner), device_id_type=MESH,
        )

    def project(b):
        here = rows_of(b)
        token = store(normed, normed_out.at[here])
        if b == 0:
            loads["kv"].wait()
        pair = jnp.dot(normed[...], wkv[...], preferred_element_type=jnp.float32).astype(jnp.bfloat16)
        for half in range(2):
            kv_part[half, here, :] = pair[:, half * HEAD_SIZE:(half + 1) * HEAD_SIZE]
        for half in range(2):
            owner, copy = kv_copy(b, half)

            @pl.when(owner != me)
            def _():
                copy.start()

            @pl.when(owner == me)
            def _():
                keyval[me // 2, here, :] = kv_part[half, here, :]
        if b == 0:
            loads["q"].wait()

        @pl.loop(0, q.shape[1] // TILE)
        def _(n):
            cols = pl.ds(pl.multiple_of(n * TILE, TILE), TILE)
            q[here, cols] = jnp.dot(
                normed[...], wq[:, cols], preferred_element_type=jnp.float32
            ).astype(jnp.bfloat16)

        return token

    def receive_kv(b):
        for kind, own in ((0, 0), (1, 3)):

            @pl.when(me != own)
            def _():
                pltpu.make_async_remote_copy(
                    src_ref=kv_part.at[0, rows_of(b)], dst_ref=keyval.at[kind, rows_of(b)],
                    send_sem=kv_send.at[0, b], recv_sem=kv_recv.at[kind, b],
                    device_id=beside, device_id_type=MESH,
                ).wait_recv()

    def attention(b, first, last):
        start, stop = b * BLOCK_ROWS, (b + 1) * BLOCK_ROWS
        here = slice(start, stop)

        @pl.loop(first, last)
        def _(h):
            cols = pl.ds(pl.multiple_of(h * HEAD_SIZE, HEAD_SIZE), HEAD_SIZE)
            scores = dot(q[here, cols], keyval[0, :stop, :], NT) * (HEAD_SIZE ** (-0.5))
            row_ids = lax.broadcasted_iota(jnp.int32, scores.shape, 0) + start
            col_ids = lax.broadcasted_iota(jnp.int32, scores.shape, 1)
            scores = jnp.where(row_ids >= col_ids, scores, jnp.float32(-1e30))
            top = jnp.max(scores, axis=-1, keepdims=True)
            powers = jnp.exp(scores - top)
            share = powers * (1.0 / jnp.sum(powers, axis=-1, keepdims=True))
            share = share.astype(jnp.bfloat16)
            probs[b][h] = share
            att[here, cols] = jnp.dot(
                share, keyval[1, :stop, :], preferred_element_type=jnp.float32
            ).astype(jnp.bfloat16)

    def piece_copy(b, n):
        return pltpu.make_async_remote_copy(
            src_ref=pieces.at[n, rows_of(b)], dst_ref=arrived.at[n, rows_of(b)],
            send_sem=piece_send.at[n, b], recv_sem=piece_recv.at[n, b],
            device_id=beside, device_id_type=MESH,
        )

    near_tokens = []

    def mix(b):
        here = rows_of(b)
        if b == 0:
            loads["o"].wait()

        def term(owner, tile):
            cols = pl.ds(pl.multiple_of(owner * width + tile * TILE, TILE), TILE)
            return jnp.dot(att[here, :], wo[:, cols], preferred_element_type=jnp.float32)

        for n, owner in ((0, last_slot), (1, near_slot)):

            @pl.loop(0, width // TILE)
            def _(tile):
                cols = pl.ds(pl.multiple_of(tile * TILE, TILE), TILE)
                pieces[n, here, cols] = term(owner, tile).astype(jnp.bfloat16)

            piece_copy(b, n).start()
        piece_copy(b, 0).wait_recv()

        @pl.loop(0, width // TILE)
        def _(tile):
            cols = pl.ds(pl.multiple_of(tile * TILE, TILE), TILE)
            value = term(far_slot, tile) + arrived[0, here, cols].astype(jnp.float32)
            far[here, cols] = value.astype(jnp.bfloat16)

        piece_copy(b, 1).wait_recv()

        @pl.loop(0, width // TILE)
        def _(tile):
            cols = pl.ds(pl.multiple_of(tile * TILE, TILE), TILE)
            value = term(me, tile) + arrived[1, here, cols].astype(jnp.float32)
            near[here, cols] = value + x_all[me, here, cols].astype(jnp.float32)

        near_tokens.append(store(near.at[here], near_out.at[here]))

    def backward_in(b):
        here = rows_of(b)
        for i in range(b * per_block, (b + 1) * per_block):
            gathered(1, i)
        for p in range(parts):
            store(dy_all.at[p, here], dy_out.at[here, pl.ds(p * width, width)])

        @pl.loop(0, datt.shape[1] // TILE)
        def _(n):
            some = pl.ds(pl.multiple_of(n * TILE, TILE), TILE)
            value = jnp.zeros((BLOCK_ROWS, TILE), jnp.float32)
            for p in range(parts):
                value += dot(dy_all[p, here, :], wo[some, p * width:(p + 1) * width], NT)
            datt[here, some] = value.astype(jnp.bfloat16)

    def far_copy(b):
        return pltpu.make_async_remote_copy(
            src_ref=far.at[rows_of(b)], dst_ref=mixed_out.at[rows_of(b)],
            send_sem=far_send.at[b], recv_sem=far_recv.at[b],
            device_id=across, device_id_type=MESH,
        )

    def attention_backward(b):
        stop = (b + 1) * BLOCK_ROWS
        here = slice(b * BLOCK_ROWS, stop)

        @pl.loop(0, heads)
        def _(h):
            cols = pl.ds(pl.multiple_of(h * HEAD_SIZE, HEAD_SIZE), HEAD_SIZE)
            d_out = datt[here, cols]
            delta = jnp.sum(
                d_out.astype(jnp.float32) * att[here, cols].astype(jnp.float32), axis=-1, keepdims=True
            )
            share = probs[b][h]
            d_probs = dot(d_out, keyval[1, :stop, :], NT)
            d_scores = share.astype(jnp.float32) * (d_probs - delta) * (HEAD_SIZE ** (-0.5))
            d_scores = d_scores.astype(jnp.bfloat16)
            dq[here, cols] = jnp.dot(
                d_scores, keyval[0, :stop, :], preferred_element_type=jnp.float32
            ).astype(jnp.bfloat16)
            dk[:stop, :] += dot(d_scores, q[here, cols], TN)
            dv[:stop, :] += dot(share, d_out, TN)

    def dkv_copy(kind):
        owner, place = 2 * kind + me // 2, lax.rem(me, 2)
        columns = pl.ds(pl.multiple_of(place * HEAD_SIZE, HEAD_SIZE), HEAD_SIZE)
        return owner, columns, pltpu.make_async_remote_copy(
            src_ref=pair.at[kind], dst_ref=dkv.at[:, columns],
            send_sem=dkv_send.at[kind], recv_sem=dkv_recv.at[place],
            device_id=(section, owner), device_id_type=MESH,
        )

    def send_dkv():
        pair[0] = dk[...].astype(jnp.bfloat16)
        pair[1] = dv[...].astype(jnp.bfloat16)
        for kind in range(2):
            owner, columns, copy = dkv_copy(kind)

            @pl.when(owner != me)
            def _():
                copy.start()

            @pl.when(owner == me)
            def _():
                dkv[:, columns] = pair[kind]

    def receive_dkv():
        for place, own in ((0, 0), (1, 3)):

            @pl.when(me != own)
            def _():
                pltpu.make_async_remote_copy(
                    src_ref=pair.at[0], dst_ref=dkv.at[:, pl.ds(place * HEAD_SIZE, HEAD_SIZE)],
                    send_sem=dkv_send.at[0], recv_sem=dkv_recv.at[place],
                    device_id=beside, device_id_type=MESH,
                ).wait_recv()

    peers = (far_slot, near_slot, last_slot)

    def dot_copy(n):
        return pltpu.make_async_remote_copy(
            src_ref=dots.at[0], dst_ref=dots.at[n + 1],
            send_sem=dot_send.at[n], recv_sem=dot_recv.at[n],
            device_id=(section, peers[n]), device_id_type=MESH,
        )

    def row_dots():
        for b in range(blocks):
            here = rows_of(b)
            total = jnp.zeros((8, BLOCK_ROWS), jnp.float32)
            product = dq[here, :].astype(jnp.float32) * q[here, :].astype(jnp.float32)
            for part in (
                product,
                pair[0, here, :].astype(jnp.float32) * keyval[0, here, :].astype(jnp.float32),
                pair[1, here, :].astype(jnp.float32) * keyval[1, here, :].astype(jnp.float32),
            ):
                ones = jnp.ones((8, part.shape[1]), jnp.bfloat16)
                high = part.astype(jnp.bfloat16)
                low = (part - high.astype(jnp.float32)).astype(jnp.bfloat16)
                total += dot(ones, high, NT) + dot(ones, low, NT)
            dots[0, :, b * BLOCK_ROWS:(b + 1) * BLOCK_ROWS] = total
        for n in range(3):
            dot_copy(n).start()

    def d_copy(b, n):
        slot = me if n == 0 else far_slot
        return pltpu.make_async_remote_copy(
            src_ref=pieces.at[n, rows_of(b)], dst_ref=x_all.at[slot, rows_of(b)],
            send_sem=d_send.at[n, b], recv_sem=d_recv.at[n, b],
            device_id=beside, device_id_type=MESH,
        )

    def d_mix(b):
        here = rows_of(b)

        def term(owner, tile):
            some = pl.ds(pl.multiple_of(owner * width + tile * TILE, TILE), TILE)
            return dot(dq[here, :], wq[some, :], NT) + dot(dkv[here, :], wkv[some, :], NT)

        for n, owner in ((0, last_slot), (1, near_slot)):

            @pl.loop(0, width // TILE)
            def _(tile):
                cols = pl.ds(pl.multiple_of(tile * TILE, TILE), TILE)
                pieces[n, here, cols] = term(owner, tile).astype(jnp.bfloat16)

            d_copy(b, n).start()
        d_copy(b, 0).wait_recv()

        @pl.loop(0, width // TILE)
        def _(tile):
            cols = pl.ds(pl.multiple_of(tile * TILE, TILE), TILE)
            value = term(far_slot, tile) + x_all[near_slot, here, cols].astype(jnp.float32)
            datt[here, cols] = value.astype(jnp.bfloat16)

        store(datt.at[here], d_far_out.at[here])
        d_copy(b, 1).wait_recv()
        stored(near_tokens[b])

        @pl.loop(0, width // TILE)
        def _(tile):
            cols = pl.ds(pl.multiple_of(tile * TILE, TILE), TILE)
            near[here, cols] = term(me, tile) + x_all[last_slot, here, cols].astype(jnp.float32)

        store(near.at[here], d_near_out.at[here])

    dk[...] = jnp.zeros_like(dk)
    dv[...] = jnp.zeros_like(dv)
    relay(0, 0)
    relay(0, 1)
    relay(0, 2)
    normalise(0)
    relay(0, 3)
    normalise(1)
    token = project(0)
    relay(0, 4)
    stored(token)
    normalise(2)
    relay(0, 5)
    normalise(3)
    token = project(1)
    relay(0, 6)
    receive_kv(0)
    attention(0, 0, heads)
    stored(token)
    normalise(4)
    relay(1, 0)
    normalise(5)
    project(2)
    receive_kv(1)
    store(x_all.at[me], x_out)
    relay(1, 1)
    attention(1, 0, heads)
    relay(1, 2)
    receive_kv(2)
    attention(2, 0, heads // 2)
    relay(1, 3)
    attention(2, heads // 2, heads)
    store(att, att_out)
    relay(1, 4)
    mix(0)
    relay(1, 5)
    far_copy(0).start()
    mix(1)
    far_copy(1).start()
    relay(1, 6)
    for b in range(blocks):
        backward_in(b)
        attention_backward(b)
    send_dkv()
    mix(2)
    row_dots()
    far_copy(2).start()
    store(dq, dq_out)
    for b in range(blocks):
        for n in range(2):
            piece_copy(b, n).wait_send()
    receive_dkv()
    store(dkv, dkv_out)
    for b in range(blocks):
        d_mix(b)
    total = dots[0]
    for n in range(3):
        dot_copy(n).wait_recv()
        total += dots[n + 1]
    dot_ref[...] = total

    for a in range(2):
        for kind in range(4):
            for i in range(chunks):
                move(a, kind, i).wait_send()
    for b in range(blocks):
        for half in range(2):
            owner, copy = kv_copy(b, half)

            @pl.when(owner != me)
            def _():
                copy.wait_send()
        for n in range(2):
            d_copy(b, n).wait_send()
        far_copy(b).wait()
    for kind in range(2):
        owner, _, copy = dkv_copy(kind)

        @pl.when(owner != me)
        def _():
            copy.wait_send()
    for n in range(3):
        dot_copy(n).wait_send()
    for n, copy in enumerate(stores):
        if n not in waited:
            copy.wait()


def layer(x_handed, cot_handed, w_query, key_value_weight, w_out, norm_gain):
    rows, width = x_handed.shape[1:]
    features, heads = w_query.shape[1], w_query.shape[2] // HEAD_SIZE
    inner = heads * HEAD_SIZE
    chunks, blocks = rows // CHUNK, rows // BLOCK_ROWS
    parts = features // width
    bf16, f32 = jnp.bfloat16, jnp.float32
    anywhere = pl.BlockSpec(memory_space=pl.ANY)
    local = pl.BlockSpec(memory_space=pltpu.VMEM)
    dma = pltpu.SemaphoreType.DMA
    kv_rows = (2, rows, HEAD_SIZE)
    shapes = [
        ((rows, width), bf16), ((rows, features), bf16), ((rows, features), bf16), ((rows, 128), f32),
        ((rows, inner), bf16), ((rows, width), bf16), ((rows, width), f32), ((rows, inner), bf16),
        ((rows, 2 * HEAD_SIZE), bf16), ((rows, width), bf16), ((rows, width), f32), ((8, rows), f32),
    ]
    return pl.pallas_call(
        layer_kernel,
        out_shape=[jax.ShapeDtypeStruct(*s) for s in shapes],
        in_specs=[anywhere] * 5 + [local],
        out_specs=[local if n in (3, 11) else anywhere for n in range(len(shapes))],
        scratch_shapes=[
            pltpu.VMEM((parts, rows, width), bf16),
            pltpu.VMEM((parts, rows, width), bf16),
            pltpu.VMEM(w_query.shape[1:], bf16),
            pltpu.VMEM(key_value_weight.shape[1:], bf16),
            pltpu.VMEM(w_out.shape[1:], bf16),
            pltpu.VMEM((BLOCK_ROWS, features), bf16),
            pltpu.VMEM((rows, inner), bf16),
            pltpu.VMEM(kv_rows, bf16),
            pltpu.VMEM(kv_rows, bf16),
            pltpu.VMEM((rows, inner), bf16),
        ]
        + [pltpu.VMEM((heads, BLOCK_ROWS, (b + 1) * BLOCK_ROWS), bf16) for b in range(blocks)]
        + [
            pltpu.VMEM((rows, inner), bf16),
            pltpu.VMEM((2, rows, width), bf16),
            pltpu.VMEM((2, rows, width), bf16),
            pltpu.VMEM((rows, width), bf16),
            pltpu.VMEM((rows, width), f32),
            pltpu.VMEM((rows, inner), bf16),
            pltpu.VMEM((rows, HEAD_SIZE), f32),
            pltpu.VMEM((rows, HEAD_SIZE), f32),
            pltpu.VMEM(kv_rows, bf16),
            pltpu.VMEM((rows, 2 * HEAD_SIZE), bf16),
            pltpu.VMEM((4, 8, rows), f32),
            dma((3,)),
            dma((40,)),
            dma((2, 4, chunks)),
            dma((2, 4, chunks)),
            dma((2, blocks)),
            dma((2, blocks)),
            dma((2, blocks)),
            dma((2, blocks)),
            dma((blocks,)),
            dma((blocks,)),
            dma((2,)),
            dma((2,)),
            dma((2, blocks)),
            dma((2, blocks)),
            dma((3,)),
            dma((3,)),
            pltpu.SemaphoreType.REGULAR,
        ],
        compiler_params=pltpu.CompilerParams(
            collective_id=0, has_side_effects=True, vmem_limit_bytes=62 << 20
        ),
        cost_estimate=pl.CostEstimate(
            flops=14 * rows * features * inner, bytes_accessed=60 << 20, transcendentals=heads * rows * rows
        ),
    )(x_handed, cot_handed, w_query, key_value_weight, w_out, norm_gain)


def on_device(x_handed, cot_handed, w_query, key_value_weight, w_out, norm_gain):
    gain_row = norm_gain[0]
    features = gain_row.shape[0]
    me = lax.axis_index("tp")
    (
        x_part, dy_all, normed_all, inv_rms, attended, mixed_far, mixed_near,
        d_queries, d_kv_mine, d_far, d_near, row_dot,
    ) = layer(x_handed, cot_handed, w_query, key_value_weight, w_out, norm_gain)
    far_pairs = [(i, i ^ 2) for i in range(lax.axis_size("tp"))]
    d_far = lax.ppermute(d_far, "tp", far_pairs)
    layer_out = (mixed_near + mixed_far.astype(jnp.float32)).astype(jnp.bfloat16)
    grad_query = dot(normed_all, d_queries, TN).astype(jnp.bfloat16)
    grad_out = dot(attended, dy_all, TN).astype(jnp.bfloat16)
    grad_keyval = dot(normed_all, d_kv_mine, TN).astype(jnp.bfloat16)
    inv_rms = inv_rms[:, :1]
    width = x_part.shape[1]
    mine = me * width
    dy_part = lax.dynamic_slice_in_dim(dy_all, mine, width, 1)
    row_mean = (row_dot[0] / features)[:, None]
    gain_mine = lax.dynamic_slice_in_dim(gain_row, mine, width, 0)
    unit_mine = x_part.astype(jnp.float32) * inv_rms
    d_normed = d_near + d_far.astype(jnp.float32)
    grad_gain = lax.all_gather(jnp.sum(d_normed * unit_mine, axis=0), "tp", tiled=True)
    d_unit = d_normed * gain_mine
    grad_in = (
        dy_part.astype(jnp.float32) + inv_rms * (d_unit - unit_mine * row_mean)
    ).astype(jnp.bfloat16)
    return (
        layer_out[None],
        grad_in[None],
        grad_query[None],
        grad_keyval[None],
        grad_out[None],
        grad_gain[None],
    )


def on_device_any(x_handed, cot_handed, w_query, key_value_weight, w_out, norm_gain):
    x_part = shifted(x_handed, "section", 1)[0]
    dy_part = shifted(cot_handed, "section", -1)[0]
    wq_dev = w_query[0]
    wkv_dev = key_value_weight[0]
    wo_dev = w_out[0]
    gain_row = norm_gain[0]
    heads_per_device = wq_dev.shape[1] // HEAD_SIZE
    score_scale = HEAD_SIZE ** (-0.5)
    x_all = lax.all_gather(x_part, "tp", axis=1, tiled=True)
    sequence_length = x_all.shape[0]
    tok_rows = sequence_length // lax.axis_size("tp")
    row_start = lax.axis_index("tp") * tok_rows
    x_float = x_all.astype(jnp.float32)
    inv_rms = lax.rsqrt(jnp.mean(x_float * x_float, axis=-1, keepdims=True) + 1e-05)
    unit_x = x_float * inv_rms
    normed_all = (unit_x * gain_row).astype(jnp.bfloat16)
    queries = jnp.dot(normed_all, wq_dev, preferred_element_type=jnp.float32).astype(jnp.bfloat16)
    kv_part = jnp.dot(normed_all, wkv_dev, preferred_element_type=jnp.float32).astype(jnp.bfloat16)
    key_value_pairs = lax.all_gather(kv_part, "tp", axis=1, tiled=True)
    key_value_head = lax.axis_index("tp") * heads_per_device // (QUERY_HEADS // KEY_VALUE_HEADS)
    key_rows = lax.dynamic_slice_in_dim(key_value_pairs, key_value_head * HEAD_SIZE, HEAD_SIZE, 1)
    value_rows_full = lax.dynamic_slice_in_dim(
        key_value_pairs, KEY_VALUE_HEADS * HEAD_SIZE + key_value_head * HEAD_SIZE, HEAD_SIZE, 1
    )
    query_heads = queries.reshape(sequence_length, heads_per_device, HEAD_SIZE)
    scores = (
        jnp.einsum("shd,td->hst", query_heads, key_rows, preferred_element_type=jnp.float32)
        * score_scale
    )
    row_ids = lax.broadcasted_iota(jnp.int32, (sequence_length, sequence_length), 0)
    col_ids = lax.broadcasted_iota(jnp.int32, (sequence_length, sequence_length), 1)
    causal = row_ids >= col_ids
    scores = jnp.where(causal[None], scores, jnp.float32(-1e30))
    row_max = jnp.max(scores, axis=-1, keepdims=True)
    shifted_exp = jnp.exp(scores - row_max)
    attn_probs = shifted_exp / jnp.sum(shifted_exp, axis=-1, keepdims=True)
    probs_bf = attn_probs.astype(jnp.bfloat16)
    attended = jnp.einsum(
        "hst,td->shd", probs_bf, value_rows_full, preferred_element_type=jnp.float32
    ).astype(jnp.bfloat16)
    attn_flat = attended.reshape(sequence_length, heads_per_device * HEAD_SIZE)
    out_terms = jnp.dot(attn_flat, wo_dev, preferred_element_type=jnp.float32)
    mixed_part = lax.psum_scatter(
        out_terms.astype(jnp.bfloat16), "tp", scatter_dimension=1, tiled=True
    ).astype(jnp.float32)
    layer_out = (x_part.astype(jnp.float32) + mixed_part).astype(jnp.bfloat16)
    dy_all = lax.all_gather(dy_part, "tp", axis=1, tiled=True)
    grad_out = jnp.einsum(
        "sk,sd->kd", attn_flat, dy_all, preferred_element_type=jnp.float32
    ).astype(jnp.bfloat16)
    d_attended = jnp.einsum("sd,kd->sk", dy_all, wo_dev, preferred_element_type=jnp.float32).astype(
        jnp.bfloat16
    )
    d_att_heads = d_attended.reshape(sequence_length, heads_per_device, HEAD_SIZE)
    d_probs = jnp.einsum(
        "shd,td->hst", d_att_heads, value_rows_full, preferred_element_type=jnp.float32
    )
    row_delta = jnp.einsum(
        "shd,shd->hs", d_att_heads.astype(jnp.float32), attended.astype(jnp.float32)
    )
    d_scores = (attn_probs * (d_probs - row_delta[:, :, None]) * score_scale).astype(jnp.bfloat16)
    d_queries = jnp.einsum("hst,td->shd", d_scores, key_rows, preferred_element_type=jnp.float32)
    d_queries = d_queries.astype(jnp.bfloat16).reshape(
        sequence_length, heads_per_device * HEAD_SIZE
    )
    d_key_rows = jnp.einsum(
        "hst,shd->td", d_scores, query_heads, preferred_element_type=jnp.float32
    )
    value_row_gradient = jnp.einsum(
        "hst,shd->td", probs_bf, d_att_heads, preferred_element_type=jnp.float32
    )
    key_value_contribution = jnp.zeros(
        (sequence_length, 2 * KEY_VALUE_HEADS * HEAD_SIZE), jnp.float32
    )
    key_value_contribution = lax.dynamic_update_slice(
        key_value_contribution, d_key_rows, (jnp.int32(0), key_value_head * HEAD_SIZE)
    )
    key_value_contribution = lax.dynamic_update_slice(
        key_value_contribution,
        value_row_gradient,
        (jnp.int32(0), KEY_VALUE_HEADS * HEAD_SIZE + key_value_head * HEAD_SIZE),
    )
    d_keyvals = lax.psum_scatter(
        key_value_contribution.astype(jnp.bfloat16), "tp", scatter_dimension=1, tiled=True
    )
    grad_query = jnp.einsum(
        "sd,sk->dk", normed_all, d_queries, preferred_element_type=jnp.float32
    ).astype(jnp.bfloat16)
    grad_keyval = jnp.einsum(
        "sd,sk->dk", normed_all, d_keyvals, preferred_element_type=jnp.float32
    ).astype(jnp.bfloat16)
    from_query = jnp.einsum("sk,dk->sd", d_queries, wq_dev, preferred_element_type=jnp.float32)
    from_keyval = jnp.einsum("sk,dk->sd", d_keyvals, wkv_dev, preferred_element_type=jnp.float32)
    d_normed = lax.psum_scatter(
        (from_query + from_keyval).astype(jnp.bfloat16), "tp", scatter_dimension=0, tiled=True
    ).astype(jnp.float32)
    unit_rows = lax.dynamic_slice_in_dim(unit_x, row_start, tok_rows, 0)
    inv_rows = lax.dynamic_slice_in_dim(inv_rms, row_start, tok_rows, 0)
    dy_rows = lax.dynamic_slice_in_dim(dy_all, row_start, tok_rows, 0).astype(jnp.float32)
    gain_local = jnp.sum(d_normed * unit_rows, axis=0)
    grad_gain = lax.psum(gain_local, "tp")
    d_unit = d_normed * gain_row
    d_input = inv_rows * (d_unit - unit_rows * jnp.mean(d_unit * unit_rows, axis=-1, keepdims=True))
    grad_rows = (dy_rows + d_input).astype(jnp.bfloat16)
    grad_in = lax.all_to_all(grad_rows, "tp", split_axis=1, concat_axis=0, tiled=True)
    return (
        layer_out[None],
        grad_in[None],
        grad_query[None],
        grad_keyval[None],
        grad_out[None],
        grad_gain[None],
    )


def solution(mesh):
    return jax.shard_map(
        on_device if mesh.shape["tp"] == KEY_VALUE_HEADS else on_device_any,
        mesh=mesh,
        in_specs=(
            P("section", None, "tp"),
            P("section", None, "tp"),
            P("section", None, "tp"),
            P("section", None, "tp"),
            P("section", "tp", None),
            P("section", None),
        ),
        out_specs=(
            P("section", None, "tp"),
            P("section", None, "tp"),
            P("section", None, "tp"),
            P("section", None, "tp"),
            P("section", "tp", None),
            P("section", None),
        ),
        check_vma=False,
    )
```

```python
import jax
import jax.numpy as jnp
from jax import lax
from jax.experimental import pallas as pl
from jax.experimental.pallas import tpu as pltpu
from jax.sharding import PartitionSpec as P

HEAD_SIZE = 128
QUERY_HEADS = 32
KEY_VALUE_HEADS = 4


def shifted(value, axis, steps):
    count = lax.axis_size(axis)
    pairs = [(source, (source + steps) % count) for source in range(count)]
    return lax.ppermute(value, axis, pairs)


NT = (((1,), (1,)), ((), ()))
TN = (((0,), (0,)), ((), ()))
BLOCK_ROWS = 256


def dot(left, right, dims):
    return lax.dot_general(left, right, dims, preferred_element_type=jnp.float32)


MESH = pl.DeviceIdType.MESH
CHUNK = 128
TILE = 256
MIX_TILE = 1024
D_TILE = 1024


def layer_kernel(
    x_ref, dy_ref, wq_hbm, wkv_hbm, wo_hbm, gain_ref,
    x_out, dy_out, normed_out, inv_ref, att_out, mixed_out, near_out, dq_out, dkv_out, d_far_out, d_near_out, dot_ref,
    x_all, dy_all, wq, wkv, wo, normed, q, kv_part, keyval, att, probs_0, probs_1, probs_2, datt,
    pieces, arrived, far, near, dq, dk, dv, pair, dkv, dots,
    load_sem, store_sem, send_sem, recv_sem, kv_send, kv_recv, piece_send, piece_recv, far_send, far_recv,
    dkv_send, dkv_recv, d_send, d_recv, dot_send, dot_recv, credit,
):
    section, me = lax.axis_index("section"), lax.axis_index("tp")
    sections = lax.axis_size("section")
    rows, width = x_ref.shape[1], x_ref.shape[2]
    parts = x_all.shape[0]
    features = parts * width
    chunks, blocks = rows // CHUNK, rows // BLOCK_ROWS
    per_block = BLOCK_ROWS // CHUNK
    heads = q.shape[1] // HEAD_SIZE
    after, before = lax.rem(section + 1, sections), lax.rem(section + sections - 1, sections)
    far_slot, near_slot, last_slot = lax.rem(me + 2, 4), me + 1 - 2 * lax.rem(me, 2), 3 - me
    across, beside = (section, far_slot), (section, near_slot)
    shift_to = ((after, me), (before, me))
    held = (x_all, dy_all)
    probs = (probs_0, probs_1, probs_2)

    barrier = pltpu.get_barrier_semaphore()
    for peer in (across, beside, (section, last_slot), shift_to[0], shift_to[1]):
        pl.semaphore_signal(barrier, inc=1, device_id=peer, device_id_type=MESH)
    pl.semaphore_wait(barrier, 5)

    def span(i):
        return pl.ds(i * CHUNK, CHUNK)

    def rows_of(b):
        return pl.ds(b * BLOCK_ROWS, BLOCK_ROWS)

    def move(a, kind, i):
        slot = far_slot if kind == 3 else me
        target = held[a].at[slot, span(i)]
        source = (x_ref, dy_ref)[a].at[0, span(i)] if kind == 0 else target
        return pltpu.make_async_remote_copy(
            src_ref=source, dst_ref=target,
            send_sem=send_sem.at[a, kind, i], recv_sem=recv_sem.at[a, kind, i],
            device_id=(shift_to[a], across, beside, beside)[kind], device_id_type=MESH,
        )

    loads = {}
    for n, (name, source, target) in enumerate(
        (("kv", wkv_hbm, wkv), ("q", wq_hbm, wq), ("o", wo_hbm, wo))
    ):
        loads[name] = pltpu.make_async_copy(source.at[0], target, load_sem.at[n])

    stores = []

    def store(source, target):
        copy = pltpu.make_async_copy(source, target, store_sem.at[len(stores)])
        copy.start()
        stores.append(copy)
        return len(stores) - 1

    waited = set()

    def stored(*tokens):
        for n in tokens:
            stores[n].wait()
            waited.add(n)

    for i in range(chunks):
        move(0, 0, i).start()
    for name in ("kv", "q", "o"):
        loads[name].start()

    def relay(a, i):
        if i < chunks:
            move(a, 0, i).wait_recv()
            if a == 0 and i == chunks - 1:
                pl.semaphore_signal(credit, inc=1, device_id=shift_to[0], device_id_type=MESH)
            move(a, 1, i).start()
            move(a, 2, i).start()
            if a == 0 and i == chunks - 1:
                pl.semaphore_wait(credit, 1)
                for j in range(chunks):
                    move(1, 0, j).start()
        if i > 0:
            move(a, 1, i - 1).wait_recv()
            move(a, 3, i - 1).start()

    def gathered(a, i):
        move(a, 2, i).wait_recv()
        move(a, 3, i).wait_recv()

    def normalise(i):
        gathered(0, i)
        step = 32

        @pl.loop(0, CHUNK // step)
        def _(r):
            here = pl.ds(pl.multiple_of(i * CHUNK + r * step, step), step)
            local = pl.ds(pl.multiple_of((i % per_block) * CHUNK + r * step, step), step)
            total = jnp.zeros((step, 1), jnp.float32)
            for p in range(parts):
                value = x_all[p, here].astype(jnp.float32)
                total += jnp.sum(value * value, axis=-1, keepdims=True)
            inv = lax.rsqrt(total / features + 1e-05)
            inv_ref[here, :] = jnp.broadcast_to(inv, (step, inv_ref.shape[1]))
            for p in range(parts):
                value = x_all[p, here].astype(jnp.float32)
                cols = slice(p * width, (p + 1) * width)
                normed[local, cols] = (value * inv * gain_ref[0:1, cols]).astype(jnp.bfloat16)

    def kv_copy(b, half):
        owner = 2 * lax.rem(me, 2) + half
        return owner, pltpu.make_async_remote_copy(
            src_ref=kv_part.at[half, rows_of(b)], dst_ref=keyval.at[me // 2, rows_of(b)],
            send_sem=kv_send.at[half, b], recv_sem=kv_recv.at[me // 2, b],
            device_id=(section, owner), device_id_type=MESH,
        )

    def project(b):
        here = rows_of(b)
        token = store(normed, normed_out.at[here])
        if b == 0:
            loads["kv"].wait()
        pair = jnp.dot(normed[...], wkv[...], preferred_element_type=jnp.float32).astype(jnp.bfloat16)
        for half in range(2):
            kv_part[half, here, :] = pair[:, half * HEAD_SIZE:(half + 1) * HEAD_SIZE]
        for half in range(2):
            owner, copy = kv_copy(b, half)

            @pl.when(owner != me)
            def _():
                copy.start()

            @pl.when(owner == me)
            def _():
                keyval[me // 2, here, :] = kv_part[half, here, :]
        if b == 0:
            loads["q"].wait()

        @pl.loop(0, q.shape[1] // TILE, unroll=4)
        def _(n):
            cols = pl.ds(pl.multiple_of(n * TILE, TILE), TILE)
            q[here, cols] = jnp.dot(
                normed[...], wq[:, cols], preferred_element_type=jnp.float32
            ).astype(jnp.bfloat16)

        return token

    def receive_kv(b):
        for kind, own in ((0, 0), (1, 3)):

            @pl.when(me != own)
            def _():
                pltpu.make_async_remote_copy(
                    src_ref=kv_part.at[0, rows_of(b)], dst_ref=keyval.at[kind, rows_of(b)],
                    send_sem=kv_send.at[0, b], recv_sem=kv_recv.at[kind, b],
                    device_id=beside, device_id_type=MESH,
                ).wait_recv()

    def attention(b, first, last):
        start, stop = b * BLOCK_ROWS, (b + 1) * BLOCK_ROWS
        here = slice(start, stop)

        @pl.loop(first, last, unroll=4)
        def _(h):
            cols = pl.ds(pl.multiple_of(h * HEAD_SIZE, HEAD_SIZE), HEAD_SIZE)
            scores = dot(q[here, cols], keyval[0, :stop, :], NT) * (HEAD_SIZE ** (-0.5))
            row_ids = lax.broadcasted_iota(jnp.int32, scores.shape, 0) + start
            col_ids = lax.broadcasted_iota(jnp.int32, scores.shape, 1)
            scores = jnp.where(row_ids >= col_ids, scores, jnp.float32(-1e30))
            top = jnp.max(scores, axis=-1, keepdims=True)
            powers = jnp.exp(scores - top)
            share = powers * (1.0 / jnp.sum(powers, axis=-1, keepdims=True))
            share = share.astype(jnp.bfloat16)
            probs[b][h] = share
            att[here, cols] = jnp.dot(
                share, keyval[1, :stop, :], preferred_element_type=jnp.float32
            ).astype(jnp.bfloat16)

    def piece_copy(b, n):
        return pltpu.make_async_remote_copy(
            src_ref=pieces.at[n, rows_of(b)], dst_ref=arrived.at[n, rows_of(b)],
            send_sem=piece_send.at[n, b], recv_sem=piece_recv.at[n, b],
            device_id=beside, device_id_type=MESH,
        )

    near_tokens = []

    def mix(b):
        here = rows_of(b)
        if b == 0:
            loads["o"].wait()

        def term(owner, tile):
            cols = pl.ds(pl.multiple_of(owner * width + tile * MIX_TILE, MIX_TILE), MIX_TILE)
            return jnp.dot(att[here, :], wo[:, cols], preferred_element_type=jnp.float32)

        for n, owner in ((0, last_slot), (1, near_slot)):

            @pl.loop(0, width // MIX_TILE)
            def _(tile):
                cols = pl.ds(pl.multiple_of(tile * MIX_TILE, MIX_TILE), MIX_TILE)
                pieces[n, here, cols] = term(owner, tile).astype(jnp.bfloat16)

            piece_copy(b, n).start()
        piece_copy(b, 0).wait_recv()

        @pl.loop(0, width // MIX_TILE)
        def _(tile):
            cols = pl.ds(pl.multiple_of(tile * MIX_TILE, MIX_TILE), MIX_TILE)
            value = term(far_slot, tile) + arrived[0, here, cols].astype(jnp.float32)
            far[here, cols] = value.astype(jnp.bfloat16)

        piece_copy(b, 1).wait_recv()

        @pl.loop(0, width // MIX_TILE)
        def _(tile):
            cols = pl.ds(pl.multiple_of(tile * MIX_TILE, MIX_TILE), MIX_TILE)
            value = term(me, tile) + arrived[1, here, cols].astype(jnp.float32)
            near[here, cols] = value + x_all[me, here, cols].astype(jnp.float32)

        near_tokens.append(store(near.at[here], near_out.at[here]))

    def backward_in(b):
        here = rows_of(b)
        for i in range(b * per_block, (b + 1) * per_block):
            gathered(1, i)
        for p in range(parts):
            store(dy_all.at[p, here], dy_out.at[here, pl.ds(p * width, width)])

        @pl.loop(0, datt.shape[1] // TILE, unroll=4)
        def _(n):
            some = pl.ds(pl.multiple_of(n * TILE, TILE), TILE)
            value = jnp.zeros((BLOCK_ROWS, TILE), jnp.float32)
            for p in range(parts):
                value += dot(dy_all[p, here, :], wo[some, p * width:(p + 1) * width], NT)
            datt[here, some] = value.astype(jnp.bfloat16)

    def far_copy(b):
        return pltpu.make_async_remote_copy(
            src_ref=far.at[rows_of(b)], dst_ref=mixed_out.at[rows_of(b)],
            send_sem=far_send.at[b], recv_sem=far_recv.at[b],
            device_id=across, device_id_type=MESH,
        )

    def attention_backward(b):
        stop = (b + 1) * BLOCK_ROWS
        here = slice(b * BLOCK_ROWS, stop)

        @pl.loop(0, heads, unroll=4)
        def _(h):
            cols = pl.ds(pl.multiple_of(h * HEAD_SIZE, HEAD_SIZE), HEAD_SIZE)
            d_out = datt[here, cols]
            delta = jnp.sum(
                d_out.astype(jnp.float32) * att[here, cols].astype(jnp.float32), axis=-1, keepdims=True
            )
            share = probs[b][h]
            d_probs = dot(d_out, keyval[1, :stop, :], NT)
            d_scores = share.astype(jnp.float32) * (d_probs - delta) * (HEAD_SIZE ** (-0.5))
            d_scores = d_scores.astype(jnp.bfloat16)
            dq[here, cols] = jnp.dot(
                d_scores, keyval[0, :stop, :], preferred_element_type=jnp.float32
            ).astype(jnp.bfloat16)
            dk[:stop, :] += dot(d_scores, q[here, cols], TN)
            dv[:stop, :] += dot(share, d_out, TN)

    def dkv_copy(kind):
        owner, place = 2 * kind + me // 2, lax.rem(me, 2)
        columns = pl.ds(pl.multiple_of(place * HEAD_SIZE, HEAD_SIZE), HEAD_SIZE)
        return owner, columns, pltpu.make_async_remote_copy(
            src_ref=pair.at[kind], dst_ref=dkv.at[:, columns],
            send_sem=dkv_send.at[kind], recv_sem=dkv_recv.at[place],
            device_id=(section, owner), device_id_type=MESH,
        )

    def send_dkv():
        pair[0] = dk[...].astype(jnp.bfloat16)
        pair[1] = dv[...].astype(jnp.bfloat16)
        for kind in range(2):
            owner, columns, copy = dkv_copy(kind)

            @pl.when(owner != me)
            def _():
                copy.start()

            @pl.when(owner == me)
            def _():
                dkv[:, columns] = pair[kind]

    def receive_dkv():
        for place, own in ((0, 0), (1, 3)):

            @pl.when(me != own)
            def _():
                pltpu.make_async_remote_copy(
                    src_ref=pair.at[0], dst_ref=dkv.at[:, pl.ds(place * HEAD_SIZE, HEAD_SIZE)],
                    send_sem=dkv_send.at[0], recv_sem=dkv_recv.at[place],
                    device_id=beside, device_id_type=MESH,
                ).wait_recv()

    peers = (far_slot, near_slot, last_slot)

    def dot_copy(n):
        return pltpu.make_async_remote_copy(
            src_ref=dots.at[0], dst_ref=dots.at[n + 1],
            send_sem=dot_send.at[n], recv_sem=dot_recv.at[n],
            device_id=(section, peers[n]), device_id_type=MESH,
        )

    def row_dots():
        for b in range(blocks):
            here = rows_of(b)
            total = jnp.zeros((8, BLOCK_ROWS), jnp.float32)
            product = dq[here, :].astype(jnp.float32) * q[here, :].astype(jnp.float32)
            for part in (
                product,
                pair[0, here, :].astype(jnp.float32) * keyval[0, here, :].astype(jnp.float32),
                pair[1, here, :].astype(jnp.float32) * keyval[1, here, :].astype(jnp.float32),
            ):
                ones = jnp.ones((8, part.shape[1]), jnp.bfloat16)
                high = part.astype(jnp.bfloat16)
                low = (part - high.astype(jnp.float32)).astype(jnp.bfloat16)
                total += dot(ones, high, NT) + dot(ones, low, NT)
            dots[0, :, b * BLOCK_ROWS:(b + 1) * BLOCK_ROWS] = total
        for n in range(3):
            dot_copy(n).start()

    def d_copy(b, n):
        slot = me if n == 0 else far_slot
        return pltpu.make_async_remote_copy(
            src_ref=pieces.at[n, rows_of(b)], dst_ref=x_all.at[slot, rows_of(b)],
            send_sem=d_send.at[n, b], recv_sem=d_recv.at[n, b],
            device_id=beside, device_id_type=MESH,
        )

    def d_mix(b):
        here = rows_of(b)

        def term(owner, tile):
            some = pl.ds(pl.multiple_of(owner * width + tile * D_TILE, D_TILE), D_TILE)
            return dot(dq[here, :], wq[some, :], NT) + dot(dkv[here, :], wkv[some, :], NT)

        for n, owner in ((0, last_slot), (1, near_slot)):

            @pl.loop(0, width // D_TILE)
            def _(tile):
                cols = pl.ds(pl.multiple_of(tile * D_TILE, D_TILE), D_TILE)
                pieces[n, here, cols] = term(owner, tile).astype(jnp.bfloat16)

            d_copy(b, n).start()
        d_copy(b, 0).wait_recv()

        @pl.loop(0, width // D_TILE)
        def _(tile):
            cols = pl.ds(pl.multiple_of(tile * D_TILE, D_TILE), D_TILE)
            value = term(far_slot, tile) + x_all[near_slot, here, cols].astype(jnp.float32)
            datt[here, cols] = value.astype(jnp.bfloat16)

        store(datt.at[here], d_far_out.at[here])
        d_copy(b, 1).wait_recv()
        stored(near_tokens[b])

        @pl.loop(0, width // D_TILE)
        def _(tile):
            cols = pl.ds(pl.multiple_of(tile * D_TILE, D_TILE), D_TILE)
            near[here, cols] = term(me, tile) + x_all[last_slot, here, cols].astype(jnp.float32)

        store(near.at[here], d_near_out.at[here])

    dk[...] = jnp.zeros_like(dk)
    dv[...] = jnp.zeros_like(dv)
    relay(0, 0)
    relay(0, 1)
    relay(0, 2)
    normalise(0)
    relay(0, 3)
    normalise(1)
    token = project(0)
    relay(0, 4)
    stored(token)
    normalise(2)
    relay(0, 5)
    normalise(3)
    token = project(1)
    relay(0, 6)
    receive_kv(0)
    attention(0, 0, heads)
    stored(token)
    normalise(4)
    relay(1, 0)
    normalise(5)
    project(2)
    receive_kv(1)
    store(x_all.at[me], x_out)
    relay(1, 1)
    attention(1, 0, heads)
    relay(1, 2)
    receive_kv(2)
    attention(2, 0, heads // 2)
    relay(1, 3)
    attention(2, heads // 2, heads)
    store(att, att_out)
    relay(1, 4)
    mix(0)
    relay(1, 5)
    far_copy(0).start()
    mix(1)
    far_copy(1).start()
    relay(1, 6)
    for b in range(blocks):
        backward_in(b)
        attention_backward(b)
    send_dkv()
    mix(2)
    row_dots()
    far_copy(2).start()
    store(dq, dq_out)
    for b in range(blocks):
        for n in range(2):
            piece_copy(b, n).wait_send()
    receive_dkv()
    store(dkv, dkv_out)
    for b in range(blocks):
        d_mix(b)
    total = dots[0]
    for n in range(3):
        dot_copy(n).wait_recv()
        total += dots[n + 1]
    dot_ref[...] = total

    for a in range(2):
        for kind in range(4):
            for i in range(chunks):
                move(a, kind, i).wait_send()
    for b in range(blocks):
        for half in range(2):
            owner, copy = kv_copy(b, half)

            @pl.when(owner != me)
            def _():
                copy.wait_send()
        for n in range(2):
            d_copy(b, n).wait_send()
        far_copy(b).wait()
    for kind in range(2):
        owner, _, copy = dkv_copy(kind)

        @pl.when(owner != me)
        def _():
            copy.wait_send()
    for n in range(3):
        dot_copy(n).wait_send()
    for n, copy in enumerate(stores):
        if n not in waited:
            copy.wait()


def layer(x_handed, cot_handed, w_query, key_value_weight, w_out, norm_gain):
    rows, width = x_handed.shape[1:]
    features, heads = w_query.shape[1], w_query.shape[2] // HEAD_SIZE
    inner = heads * HEAD_SIZE
    chunks, blocks = rows // CHUNK, rows // BLOCK_ROWS
    parts = features // width
    bf16, f32 = jnp.bfloat16, jnp.float32
    anywhere = pl.BlockSpec(memory_space=pl.ANY)
    local = pl.BlockSpec(memory_space=pltpu.VMEM)
    dma = pltpu.SemaphoreType.DMA
    kv_rows = (2, rows, HEAD_SIZE)
    shapes = [
        ((rows, width), bf16), ((rows, features), bf16), ((rows, features), bf16), ((rows, 128), f32),
        ((rows, inner), bf16), ((rows, width), bf16), ((rows, width), f32), ((rows, inner), bf16),
        ((rows, 2 * HEAD_SIZE), bf16), ((rows, width), bf16), ((rows, width), f32), ((8, rows), f32),
    ]
    return pl.pallas_call(
        layer_kernel,
        out_shape=[jax.ShapeDtypeStruct(*s) for s in shapes],
        in_specs=[anywhere] * 5 + [local],
        out_specs=[local if n in (3, 11) else anywhere for n in range(len(shapes))],
        scratch_shapes=[
            pltpu.VMEM((parts, rows, width), bf16),
            pltpu.VMEM((parts, rows, width), bf16),
            pltpu.VMEM(w_query.shape[1:], bf16),
            pltpu.VMEM(key_value_weight.shape[1:], bf16),
            pltpu.VMEM(w_out.shape[1:], bf16),
            pltpu.VMEM((BLOCK_ROWS, features), bf16),
            pltpu.VMEM((rows, inner), bf16),
            pltpu.VMEM(kv_rows, bf16),
            pltpu.VMEM(kv_rows, bf16),
            pltpu.VMEM((rows, inner), bf16),
        ]
        + [pltpu.VMEM((heads, BLOCK_ROWS, (b + 1) * BLOCK_ROWS), bf16) for b in range(blocks)]
        + [
            pltpu.VMEM((rows, inner), bf16),
            pltpu.VMEM((2, rows, width), bf16),
            pltpu.VMEM((2, rows, width), bf16),
            pltpu.VMEM((rows, width), bf16),
            pltpu.VMEM((rows, width), f32),
            pltpu.VMEM((rows, inner), bf16),
            pltpu.VMEM((rows, HEAD_SIZE), f32),
            pltpu.VMEM((rows, HEAD_SIZE), f32),
            pltpu.VMEM(kv_rows, bf16),
            pltpu.VMEM((rows, 2 * HEAD_SIZE), bf16),
            pltpu.VMEM((4, 8, rows), f32),
            dma((3,)),
            dma((40,)),
            dma((2, 4, chunks)),
            dma((2, 4, chunks)),
            dma((2, blocks)),
            dma((2, blocks)),
            dma((2, blocks)),
            dma((2, blocks)),
            dma((blocks,)),
            dma((blocks,)),
            dma((2,)),
            dma((2,)),
            dma((2, blocks)),
            dma((2, blocks)),
            dma((3,)),
            dma((3,)),
            pltpu.SemaphoreType.REGULAR,
        ],
        compiler_params=pltpu.CompilerParams(
            collective_id=0, has_side_effects=True, vmem_limit_bytes=62 << 20
        ),
        cost_estimate=pl.CostEstimate(
            flops=14 * rows * features * inner, bytes_accessed=60 << 20, transcendentals=heads * rows * rows
        ),
    )(x_handed, cot_handed, w_query, key_value_weight, w_out, norm_gain)


def on_device(x_handed, cot_handed, w_query, key_value_weight, w_out, norm_gain):
    gain_row = norm_gain[0]
    features = gain_row.shape[0]
    me = lax.axis_index("tp")
    (
        x_part, dy_all, normed_all, inv_rms, attended, mixed_far, mixed_near,
        d_queries, d_kv_mine, d_far, d_near, row_dot,
    ) = layer(x_handed, cot_handed, w_query, key_value_weight, w_out, norm_gain)
    far_pairs = [(i, i ^ 2) for i in range(lax.axis_size("tp"))]
    d_far = lax.ppermute(d_far, "tp", far_pairs)
    layer_out = (mixed_near + mixed_far.astype(jnp.float32)).astype(jnp.bfloat16)
    grad_query = dot(normed_all, d_queries, TN).astype(jnp.bfloat16)
    grad_out = dot(attended, dy_all, TN).astype(jnp.bfloat16)
    grad_keyval = dot(normed_all, d_kv_mine, TN).astype(jnp.bfloat16)
    inv_rms = inv_rms[:, :1]
    width = x_part.shape[1]
    mine = me * width
    dy_part = lax.dynamic_slice_in_dim(dy_all, mine, width, 1)
    row_mean = (row_dot[0] / features)[:, None]
    gain_mine = lax.dynamic_slice_in_dim(gain_row, mine, width, 0)
    unit_mine = x_part.astype(jnp.float32) * inv_rms
    d_normed = d_near + d_far.astype(jnp.float32)
    grad_gain = lax.all_gather(jnp.sum(d_normed * unit_mine, axis=0), "tp", tiled=True)
    d_unit = d_normed * gain_mine
    grad_in = (
        dy_part.astype(jnp.float32) + inv_rms * (d_unit - unit_mine * row_mean)
    ).astype(jnp.bfloat16)
    return (
        layer_out[None],
        grad_in[None],
        grad_query[None],
        grad_keyval[None],
        grad_out[None],
        grad_gain[None],
    )


def on_device_any(x_handed, cot_handed, w_query, key_value_weight, w_out, norm_gain):
    x_part = shifted(x_handed, "section", 1)[0]
    dy_part = shifted(cot_handed, "section", -1)[0]
    wq_dev = w_query[0]
    wkv_dev = key_value_weight[0]
    wo_dev = w_out[0]
    gain_row = norm_gain[0]
    heads_per_device = wq_dev.shape[1] // HEAD_SIZE
    score_scale = HEAD_SIZE ** (-0.5)
    x_all = lax.all_gather(x_part, "tp", axis=1, tiled=True)
    sequence_length = x_all.shape[0]
    tok_rows = sequence_length // lax.axis_size("tp")
    row_start = lax.axis_index("tp") * tok_rows
    x_float = x_all.astype(jnp.float32)
    inv_rms = lax.rsqrt(jnp.mean(x_float * x_float, axis=-1, keepdims=True) + 1e-05)
    unit_x = x_float * inv_rms
    normed_all = (unit_x * gain_row).astype(jnp.bfloat16)
    queries = jnp.dot(normed_all, wq_dev, preferred_element_type=jnp.float32).astype(jnp.bfloat16)
    kv_part = jnp.dot(normed_all, wkv_dev, preferred_element_type=jnp.float32).astype(jnp.bfloat16)
    key_value_pairs = lax.all_gather(kv_part, "tp", axis=1, tiled=True)
    key_value_head = lax.axis_index("tp") * heads_per_device // (QUERY_HEADS // KEY_VALUE_HEADS)
    key_rows = lax.dynamic_slice_in_dim(key_value_pairs, key_value_head * HEAD_SIZE, HEAD_SIZE, 1)
    value_rows_full = lax.dynamic_slice_in_dim(
        key_value_pairs, KEY_VALUE_HEADS * HEAD_SIZE + key_value_head * HEAD_SIZE, HEAD_SIZE, 1
    )
    query_heads = queries.reshape(sequence_length, heads_per_device, HEAD_SIZE)
    scores = (
        jnp.einsum("shd,td->hst", query_heads, key_rows, preferred_element_type=jnp.float32)
        * score_scale
    )
    row_ids = lax.broadcasted_iota(jnp.int32, (sequence_length, sequence_length), 0)
    col_ids = lax.broadcasted_iota(jnp.int32, (sequence_length, sequence_length), 1)
    causal = row_ids >= col_ids
    scores = jnp.where(causal[None], scores, jnp.float32(-1e30))
    row_max = jnp.max(scores, axis=-1, keepdims=True)
    shifted_exp = jnp.exp(scores - row_max)
    attn_probs = shifted_exp / jnp.sum(shifted_exp, axis=-1, keepdims=True)
    probs_bf = attn_probs.astype(jnp.bfloat16)
    attended = jnp.einsum(
        "hst,td->shd", probs_bf, value_rows_full, preferred_element_type=jnp.float32
    ).astype(jnp.bfloat16)
    attn_flat = attended.reshape(sequence_length, heads_per_device * HEAD_SIZE)
    out_terms = jnp.dot(attn_flat, wo_dev, preferred_element_type=jnp.float32)
    mixed_part = lax.psum_scatter(
        out_terms.astype(jnp.bfloat16), "tp", scatter_dimension=1, tiled=True
    ).astype(jnp.float32)
    layer_out = (x_part.astype(jnp.float32) + mixed_part).astype(jnp.bfloat16)
    dy_all = lax.all_gather(dy_part, "tp", axis=1, tiled=True)
    grad_out = jnp.einsum(
        "sk,sd->kd", attn_flat, dy_all, preferred_element_type=jnp.float32
    ).astype(jnp.bfloat16)
    d_attended = jnp.einsum("sd,kd->sk", dy_all, wo_dev, preferred_element_type=jnp.float32).astype(
        jnp.bfloat16
    )
    d_att_heads = d_attended.reshape(sequence_length, heads_per_device, HEAD_SIZE)
    d_probs = jnp.einsum(
        "shd,td->hst", d_att_heads, value_rows_full, preferred_element_type=jnp.float32
    )
    row_delta = jnp.einsum(
        "shd,shd->hs", d_att_heads.astype(jnp.float32), attended.astype(jnp.float32)
    )
    d_scores = (attn_probs * (d_probs - row_delta[:, :, None]) * score_scale).astype(jnp.bfloat16)
    d_queries = jnp.einsum("hst,td->shd", d_scores, key_rows, preferred_element_type=jnp.float32)
    d_queries = d_queries.astype(jnp.bfloat16).reshape(
        sequence_length, heads_per_device * HEAD_SIZE
    )
    d_key_rows = jnp.einsum(
        "hst,shd->td", d_scores, query_heads, preferred_element_type=jnp.float32
    )
    value_row_gradient = jnp.einsum(
        "hst,shd->td", probs_bf, d_att_heads, preferred_element_type=jnp.float32
    )
    key_value_contribution = jnp.zeros(
        (sequence_length, 2 * KEY_VALUE_HEADS * HEAD_SIZE), jnp.float32
    )
    key_value_contribution = lax.dynamic_update_slice(
        key_value_contribution, d_key_rows, (jnp.int32(0), key_value_head * HEAD_SIZE)
    )
    key_value_contribution = lax.dynamic_update_slice(
        key_value_contribution,
        value_row_gradient,
        (jnp.int32(0), KEY_VALUE_HEADS * HEAD_SIZE + key_value_head * HEAD_SIZE),
    )
    d_keyvals = lax.psum_scatter(
        key_value_contribution.astype(jnp.bfloat16), "tp", scatter_dimension=1, tiled=True
    )
    grad_query = jnp.einsum(
        "sd,sk->dk", normed_all, d_queries, preferred_element_type=jnp.float32
    ).astype(jnp.bfloat16)
    grad_keyval = jnp.einsum(
        "sd,sk->dk", normed_all, d_keyvals, preferred_element_type=jnp.float32
    ).astype(jnp.bfloat16)
    from_query = jnp.einsum("sk,dk->sd", d_queries, wq_dev, preferred_element_type=jnp.float32)
    from_keyval = jnp.einsum("sk,dk->sd", d_keyvals, wkv_dev, preferred_element_type=jnp.float32)
    d_normed = lax.psum_scatter(
        (from_query + from_keyval).astype(jnp.bfloat16), "tp", scatter_dimension=0, tiled=True
    ).astype(jnp.float32)
    unit_rows = lax.dynamic_slice_in_dim(unit_x, row_start, tok_rows, 0)
    inv_rows = lax.dynamic_slice_in_dim(inv_rms, row_start, tok_rows, 0)
    dy_rows = lax.dynamic_slice_in_dim(dy_all, row_start, tok_rows, 0).astype(jnp.float32)
    gain_local = jnp.sum(d_normed * unit_rows, axis=0)
    grad_gain = lax.psum(gain_local, "tp")
    d_unit = d_normed * gain_row
    d_input = inv_rows * (d_unit - unit_rows * jnp.mean(d_unit * unit_rows, axis=-1, keepdims=True))
    grad_rows = (dy_rows + d_input).astype(jnp.bfloat16)
    grad_in = lax.all_to_all(grad_rows, "tp", split_axis=1, concat_axis=0, tiled=True)
    return (
        layer_out[None],
        grad_in[None],
        grad_query[None],
        grad_keyval[None],
        grad_out[None],
        grad_gain[None],
    )


def solution(mesh):
    return jax.shard_map(
        on_device if mesh.shape["tp"] == KEY_VALUE_HEADS else on_device_any,
        mesh=mesh,
        in_specs=(
            P("section", None, "tp"),
            P("section", None, "tp"),
            P("section", None, "tp"),
            P("section", None, "tp"),
            P("section", "tp", None),
            P("section", None),
        ),
        out_specs=(
            P("section", None, "tp"),
            P("section", None, "tp"),
            P("section", None, "tp"),
            P("section", None, "tp"),
            P("section", "tp", None),
            P("section", None),
        ),
        check_vma=False,
    )
```

```python
import jax
import jax.numpy as jnp
from jax import lax
from jax.experimental import pallas as pl
from jax.experimental.pallas import tpu as pltpu
from jax.sharding import PartitionSpec as P

HEAD_SIZE = 128
QUERY_HEADS = 32
KEY_VALUE_HEADS = 4


def shifted(value, axis, steps):
    count = lax.axis_size(axis)
    pairs = [(source, (source + steps) % count) for source in range(count)]
    return lax.ppermute(value, axis, pairs)


NT = (((1,), (1,)), ((), ()))
TN = (((0,), (0,)), ((), ()))
BLOCK_ROWS = 256


def dot(left, right, dims):
    return lax.dot_general(left, right, dims, preferred_element_type=jnp.float32)


MESH = pl.DeviceIdType.MESH
CHUNK = 128
TILE = 256
MIX_TILE = 1024
D_TILE = 1024


def layer_kernel(
    x_ref, dy_ref, wq_hbm, wkv_hbm, wo_hbm, gain_ref,
    x_out, dy_out, normed_out, inv_ref, att_out, mixed_out, near_out, dq_out, dkv_out, d_far_out, d_near_out, dot_ref,
    x_all, dy_all, wq, wkv, wo, normed, q, kv_part, keyval, att, probs_0, probs_1, probs_2, datt,
    pieces, arrived, far, near, dq, dk, dv, pair, dkv, dots,
    load_sem, store_sem, send_sem, recv_sem, kv_send, kv_recv, piece_send, piece_recv, far_send, far_recv,
    dkv_send, dkv_recv, d_send, d_recv, dot_send, dot_recv, credit,
):
    section, me = lax.axis_index("section"), lax.axis_index("tp")
    sections = lax.axis_size("section")
    rows, width = x_ref.shape[1], x_ref.shape[2]
    parts = x_all.shape[0]
    features = parts * width
    chunks, blocks = rows // CHUNK, rows // BLOCK_ROWS
    per_block = BLOCK_ROWS // CHUNK
    heads = q.shape[1] // HEAD_SIZE
    after, before = lax.rem(section + 1, sections), lax.rem(section + sections - 1, sections)
    far_slot, near_slot, last_slot = lax.rem(me + 2, 4), me + 1 - 2 * lax.rem(me, 2), 3 - me
    across, beside = (section, far_slot), (section, near_slot)
    shift_to = ((after, me), (before, me))
    held = (x_all, dy_all)
    probs = (probs_0, probs_1, probs_2)

    barrier = pltpu.get_barrier_semaphore()
    for peer in (across, beside, (section, last_slot), shift_to[0], shift_to[1]):
        pl.semaphore_signal(barrier, inc=1, device_id=peer, device_id_type=MESH)
    pl.semaphore_wait(barrier, 5)

    def span(i):
        return pl.ds(i * CHUNK, CHUNK)

    def rows_of(b):
        return pl.ds(b * BLOCK_ROWS, BLOCK_ROWS)

    def move(a, kind, i):
        slot = far_slot if kind == 3 else me
        target = held[a].at[slot, span(i)]
        source = (x_ref, dy_ref)[a].at[0, span(i)] if kind == 0 else target
        return pltpu.make_async_remote_copy(
            src_ref=source, dst_ref=target,
            send_sem=send_sem.at[a, kind, i], recv_sem=recv_sem.at[a, kind, i],
            device_id=(shift_to[a], across, beside, beside)[kind], device_id_type=MESH,
        )

    loads = {}
    for n, (name, source, target) in enumerate(
        (("kv", wkv_hbm, wkv), ("q", wq_hbm, wq), ("o", wo_hbm, wo))
    ):
        loads[name] = pltpu.make_async_copy(source.at[0], target, load_sem.at[n])

    stores = []

    def store(source, target):
        copy = pltpu.make_async_copy(source, target, store_sem.at[len(stores)])
        copy.start()
        stores.append(copy)
        return len(stores) - 1

    waited = set()

    def stored(*tokens):
        for n in tokens:
            stores[n].wait()
            waited.add(n)

    for i in range(chunks):
        move(0, 0, i).start()
    for name in ("kv", "q", "o"):
        loads[name].start()

    def relay(a, i):
        if i < chunks:
            move(a, 0, i).wait_recv()
            if a == 0 and i == chunks - 1:
                pl.semaphore_signal(credit, inc=1, device_id=shift_to[0], device_id_type=MESH)
            move(a, 1, i).start()
            move(a, 2, i).start()
            if a == 0 and i == chunks - 1:
                pl.semaphore_wait(credit, 1)
                for j in range(chunks):
                    move(1, 0, j).start()
        if i > 0:
            move(a, 1, i - 1).wait_recv()
            move(a, 3, i - 1).start()

    def gathered(a, i):
        move(a, 2, i).wait_recv()
        move(a, 3, i).wait_recv()

    def normalise(i):
        gathered(0, i)
        step = 32

        @pl.loop(0, CHUNK // step)
        def _(r):
            here = pl.ds(pl.multiple_of(i * CHUNK + r * step, step), step)
            local = pl.ds(pl.multiple_of((i % per_block) * CHUNK + r * step, step), step)
            total = jnp.zeros((step, 1), jnp.float32)
            for p in range(parts):
                value = x_all[p, here].astype(jnp.float32)
                total += jnp.sum(value * value, axis=-1, keepdims=True)
            inv = lax.rsqrt(total / features + 1e-05)
            inv_ref[here, :] = jnp.broadcast_to(inv, (step, inv_ref.shape[1]))
            for p in range(parts):
                value = x_all[p, here].astype(jnp.float32)
                cols = slice(p * width, (p + 1) * width)
                normed[local, cols] = (value * inv * gain_ref[0:1, cols]).astype(jnp.bfloat16)

    def kv_copy(b, half):
        owner = 2 * lax.rem(me, 2) + half
        return owner, pltpu.make_async_remote_copy(
            src_ref=kv_part.at[half, rows_of(b)], dst_ref=keyval.at[me // 2, rows_of(b)],
            send_sem=kv_send.at[half, b], recv_sem=kv_recv.at[me // 2, b],
            device_id=(section, owner), device_id_type=MESH,
        )

    def project(b):
        here = rows_of(b)
        token = store(normed, normed_out.at[here])
        if b == 0:
            loads["kv"].wait()
        pair = jnp.dot(normed[...], wkv[...], preferred_element_type=jnp.float32).astype(jnp.bfloat16)
        for half in range(2):
            kv_part[half, here, :] = pair[:, half * HEAD_SIZE:(half + 1) * HEAD_SIZE]
        for half in range(2):
            owner, copy = kv_copy(b, half)

            @pl.when(owner != me)
            def _():
                copy.start()

            @pl.when(owner == me)
            def _():
                keyval[me // 2, here, :] = kv_part[half, here, :]
        if b == 0:
            loads["q"].wait()

        @pl.loop(0, q.shape[1] // TILE, unroll=4)
        def _(n):
            cols = pl.ds(pl.multiple_of(n * TILE, TILE), TILE)
            q[here, cols] = jnp.dot(
                normed[...], wq[:, cols], preferred_element_type=jnp.float32
            ).astype(jnp.bfloat16)

        return token

    def receive_kv(b):
        for kind, own in ((0, 0), (1, 3)):

            @pl.when(me != own)
            def _():
                pltpu.make_async_remote_copy(
                    src_ref=kv_part.at[0, rows_of(b)], dst_ref=keyval.at[kind, rows_of(b)],
                    send_sem=kv_send.at[0, b], recv_sem=kv_recv.at[kind, b],
                    device_id=beside, device_id_type=MESH,
                ).wait_recv()

    def attention(b, first, last):
        start, stop = b * BLOCK_ROWS, (b + 1) * BLOCK_ROWS
        here = slice(start, stop)

        @pl.loop(first, last, unroll=4)
        def _(h):
            cols = pl.ds(pl.multiple_of(h * HEAD_SIZE, HEAD_SIZE), HEAD_SIZE)
            scores = dot(q[here, cols], keyval[0, :stop, :], NT) * (HEAD_SIZE ** (-0.5))
            row_ids = lax.broadcasted_iota(jnp.int32, scores.shape, 0) + start
            col_ids = lax.broadcasted_iota(jnp.int32, scores.shape, 1)
            scores = jnp.where(row_ids >= col_ids, scores, jnp.float32(-1e30))
            top = jnp.max(scores, axis=-1, keepdims=True)
            powers = jnp.exp(scores - top)
            share = powers * (1.0 / jnp.sum(powers, axis=-1, keepdims=True))
            share = share.astype(jnp.bfloat16)
            probs[b][h] = share
            att[here, cols] = jnp.dot(
                share, keyval[1, :stop, :], preferred_element_type=jnp.float32
            ).astype(jnp.bfloat16)

    def piece_copy(b, n):
        return pltpu.make_async_remote_copy(
            src_ref=pieces.at[n, rows_of(b)], dst_ref=arrived.at[n, rows_of(b)],
            send_sem=piece_send.at[n, b], recv_sem=piece_recv.at[n, b],
            device_id=beside, device_id_type=MESH,
        )

    near_tokens = []

    def out_term(b, owner, tile):
        cols = pl.ds(pl.multiple_of(owner * width + tile * MIX_TILE, MIX_TILE), MIX_TILE)
        return jnp.dot(att[rows_of(b), :], wo[:, cols], preferred_element_type=jnp.float32)

    def mix_send(b):
        here = rows_of(b)
        if b == 0:
            loads["o"].wait()

        for n, owner in ((0, last_slot), (1, near_slot)):

            @pl.loop(0, width // MIX_TILE)
            def _(tile):
                cols = pl.ds(pl.multiple_of(tile * MIX_TILE, MIX_TILE), MIX_TILE)
                pieces[n, here, cols] = out_term(b, owner, tile).astype(jnp.bfloat16)

            piece_copy(b, n).start()

    def mix_receive(b):
        here = rows_of(b)
        piece_copy(b, 0).wait_recv()

        @pl.loop(0, width // MIX_TILE)
        def _(tile):
            cols = pl.ds(pl.multiple_of(tile * MIX_TILE, MIX_TILE), MIX_TILE)
            value = out_term(b, far_slot, tile) + arrived[0, here, cols].astype(jnp.float32)
            far[here, cols] = value.astype(jnp.bfloat16)

        if b < blocks - 1:
            far_copy(b).start()
        piece_copy(b, 1).wait_recv()

        @pl.loop(0, width // MIX_TILE)
        def _(tile):
            cols = pl.ds(pl.multiple_of(tile * MIX_TILE, MIX_TILE), MIX_TILE)
            value = out_term(b, me, tile) + arrived[1, here, cols].astype(jnp.float32)
            near[here, cols] = value + x_all[me, here, cols].astype(jnp.float32)

        near_tokens.append(store(near.at[here], near_out.at[here]))

    def backward_in(b):
        here = rows_of(b)
        for i in range(b * per_block, (b + 1) * per_block):
            gathered(1, i)
        for p in range(parts):
            store(dy_all.at[p, here], dy_out.at[here, pl.ds(p * width, width)])

        @pl.loop(0, datt.shape[1] // TILE, unroll=4)
        def _(n):
            some = pl.ds(pl.multiple_of(n * TILE, TILE), TILE)
            value = jnp.zeros((BLOCK_ROWS, TILE), jnp.float32)
            for p in range(parts):
                value += dot(dy_all[p, here, :], wo[some, p * width:(p + 1) * width], NT)
            datt[here, some] = value.astype(jnp.bfloat16)

    def far_copy(b):
        return pltpu.make_async_remote_copy(
            src_ref=far.at[rows_of(b)], dst_ref=mixed_out.at[rows_of(b)],
            send_sem=far_send.at[b], recv_sem=far_recv.at[b],
            device_id=across, device_id_type=MESH,
        )

    def attention_backward(b):
        stop = (b + 1) * BLOCK_ROWS
        here = slice(b * BLOCK_ROWS, stop)

        @pl.loop(0, heads, unroll=4)
        def _(h):
            cols = pl.ds(pl.multiple_of(h * HEAD_SIZE, HEAD_SIZE), HEAD_SIZE)
            d_out = datt[here, cols]
            delta = jnp.sum(
                d_out.astype(jnp.float32) * att[here, cols].astype(jnp.float32), axis=-1, keepdims=True
            )
            share = probs[b][h]
            d_probs = dot(d_out, keyval[1, :stop, :], NT)
            d_scores = share.astype(jnp.float32) * (d_probs - delta) * (HEAD_SIZE ** (-0.5))
            d_scores = d_scores.astype(jnp.bfloat16)
            dq[here, cols] = jnp.dot(
                d_scores, keyval[0, :stop, :], preferred_element_type=jnp.float32
            ).astype(jnp.bfloat16)
            dk[:stop, :] += dot(d_scores, q[here, cols], TN)
            dv[:stop, :] += dot(share, d_out, TN)

    def dkv_copy(kind):
        owner, place = 2 * kind + me // 2, lax.rem(me, 2)
        columns = pl.ds(pl.multiple_of(place * HEAD_SIZE, HEAD_SIZE), HEAD_SIZE)
        return owner, columns, pltpu.make_async_remote_copy(
            src_ref=pair.at[kind], dst_ref=dkv.at[:, columns],
            send_sem=dkv_send.at[kind], recv_sem=dkv_recv.at[place],
            device_id=(section, owner), device_id_type=MESH,
        )

    def send_dkv():
        pair[0] = dk[...].astype(jnp.bfloat16)
        pair[1] = dv[...].astype(jnp.bfloat16)
        for kind in range(2):
            owner, columns, copy = dkv_copy(kind)

            @pl.when(owner != me)
            def _():
                copy.start()

            @pl.when(owner == me)
            def _():
                dkv[:, columns] = pair[kind]

    def receive_dkv():
        for place, own in ((0, 0), (1, 3)):

            @pl.when(me != own)
            def _():
                pltpu.make_async_remote_copy(
                    src_ref=pair.at[0], dst_ref=dkv.at[:, pl.ds(place * HEAD_SIZE, HEAD_SIZE)],
                    send_sem=dkv_send.at[0], recv_sem=dkv_recv.at[place],
                    device_id=beside, device_id_type=MESH,
                ).wait_recv()

    peers = (far_slot, near_slot, last_slot)

    def dot_copy(n):
        return pltpu.make_async_remote_copy(
            src_ref=dots.at[0], dst_ref=dots.at[n + 1],
            send_sem=dot_send.at[n], recv_sem=dot_recv.at[n],
            device_id=(section, peers[n]), device_id_type=MESH,
        )

    def row_dots():
        for b in range(blocks):
            here = rows_of(b)
            total = jnp.zeros((8, BLOCK_ROWS), jnp.float32)
            product = dq[here, :].astype(jnp.float32) * q[here, :].astype(jnp.float32)
            for part in (
                product,
                pair[0, here, :].astype(jnp.float32) * keyval[0, here, :].astype(jnp.float32),
                pair[1, here, :].astype(jnp.float32) * keyval[1, here, :].astype(jnp.float32),
            ):
                ones = jnp.ones((8, part.shape[1]), jnp.bfloat16)
                high = part.astype(jnp.bfloat16)
                low = (part - high.astype(jnp.float32)).astype(jnp.bfloat16)
                total += dot(ones, high, NT) + dot(ones, low, NT)
            dots[0, :, b * BLOCK_ROWS:(b + 1) * BLOCK_ROWS] = total
        for n in range(3):
            dot_copy(n).start()

    def d_copy(b, n):
        slot = me if n == 0 else far_slot
        return pltpu.make_async_remote_copy(
            src_ref=pieces.at[n, rows_of(b)], dst_ref=x_all.at[slot, rows_of(b)],
            send_sem=d_send.at[n, b], recv_sem=d_recv.at[n, b],
            device_id=beside, device_id_type=MESH,
        )

    def in_term(b, owner, tile):
        here = rows_of(b)
        some = pl.ds(pl.multiple_of(owner * width + tile * D_TILE, D_TILE), D_TILE)
        return dot(dq[here, :], wq[some, :], NT) + dot(dkv[here, :], wkv[some, :], NT)

    def in_scatter(b):
        here = rows_of(b)

        for n, owner in ((0, last_slot), (1, near_slot)):

            @pl.loop(0, width // D_TILE)
            def _(tile):
                cols = pl.ds(pl.multiple_of(tile * D_TILE, D_TILE), D_TILE)
                pieces[n, here, cols] = in_term(b, owner, tile).astype(jnp.bfloat16)

            d_copy(b, n).start()

    def in_collect(b):
        here = rows_of(b)
        d_copy(b, 0).wait_recv()

        @pl.loop(0, width // D_TILE)
        def _(tile):
            cols = pl.ds(pl.multiple_of(tile * D_TILE, D_TILE), D_TILE)
            value = in_term(b, far_slot, tile) + x_all[near_slot, here, cols].astype(jnp.float32)
            datt[here, cols] = value.astype(jnp.bfloat16)

        store(datt.at[here], d_far_out.at[here])
        d_copy(b, 1).wait_recv()
        stored(near_tokens[b])

        @pl.loop(0, width // D_TILE)
        def _(tile):
            cols = pl.ds(pl.multiple_of(tile * D_TILE, D_TILE), D_TILE)
            near[here, cols] = in_term(b, me, tile) + x_all[last_slot, here, cols].astype(jnp.float32)

        store(near.at[here], d_near_out.at[here])

    dk[...] = jnp.zeros_like(dk)
    dv[...] = jnp.zeros_like(dv)
    relay(0, 0)
    relay(0, 1)
    relay(0, 2)
    relay(0, 3)
    normalise(0)
    relay(0, 4)
    normalise(1)
    token = project(0)
    relay(0, 5)
    stored(token)
    normalise(2)
    relay(0, 6)
    normalise(3)
    token = project(1)
    receive_kv(0)
    relay(1, 0)
    attention(0, 0, heads)
    stored(token)
    normalise(4)
    relay(1, 1)
    normalise(5)
    project(2)
    store(x_all.at[me], x_out)
    relay(1, 2)
    receive_kv(1)
    attention(1, 0, heads)
    relay(1, 3)
    receive_kv(2)
    attention(2, 0, heads // 2)
    relay(1, 4)
    attention(2, heads // 2, heads)
    store(att, att_out)
    relay(1, 5)
    mix_send(0)
    mix_send(1)
    mix_receive(0)
    relay(1, 6)
    mix_receive(1)
    for b in range(blocks):
        backward_in(b)
        attention_backward(b)
    send_dkv()
    mix_send(2)
    mix_receive(2)
    row_dots()
    far_copy(2).start()
    store(dq, dq_out)
    for b in range(blocks):
        for n in range(2):
            piece_copy(b, n).wait_send()
    receive_dkv()
    store(dkv, dkv_out)
    for b in range(blocks):
        in_scatter(b)
    for b in range(blocks):
        in_collect(b)
    total = dots[0]
    for n in range(3):
        dot_copy(n).wait_recv()
        total += dots[n + 1]
    dot_ref[...] = total

    for a in range(2):
        for kind in range(4):
            for i in range(chunks):
                move(a, kind, i).wait_send()
    for b in range(blocks):
        for half in range(2):
            owner, copy = kv_copy(b, half)

            @pl.when(owner != me)
            def _():
                copy.wait_send()
        for n in range(2):
            d_copy(b, n).wait_send()
        far_copy(b).wait()
    for kind in range(2):
        owner, _, copy = dkv_copy(kind)

        @pl.when(owner != me)
        def _():
            copy.wait_send()
    for n in range(3):
        dot_copy(n).wait_send()
    for n, copy in enumerate(stores):
        if n not in waited:
            copy.wait()


def layer(x_handed, cot_handed, w_query, key_value_weight, w_out, norm_gain):
    rows, width = x_handed.shape[1:]
    features, heads = w_query.shape[1], w_query.shape[2] // HEAD_SIZE
    inner = heads * HEAD_SIZE
    chunks, blocks = rows // CHUNK, rows // BLOCK_ROWS
    parts = features // width
    bf16, f32 = jnp.bfloat16, jnp.float32
    anywhere = pl.BlockSpec(memory_space=pl.ANY)
    local = pl.BlockSpec(memory_space=pltpu.VMEM)
    dma = pltpu.SemaphoreType.DMA
    kv_rows = (2, rows, HEAD_SIZE)
    shapes = [
        ((rows, width), bf16), ((rows, features), bf16), ((rows, features), bf16), ((rows, 128), f32),
        ((rows, inner), bf16), ((rows, width), bf16), ((rows, width), f32), ((rows, inner), bf16),
        ((rows, 2 * HEAD_SIZE), bf16), ((rows, width), bf16), ((rows, width), f32), ((8, rows), f32),
    ]
    return pl.pallas_call(
        layer_kernel,
        out_shape=[jax.ShapeDtypeStruct(*s) for s in shapes],
        in_specs=[anywhere] * 5 + [local],
        out_specs=[local if n in (3, 11) else anywhere for n in range(len(shapes))],
        scratch_shapes=[
            pltpu.VMEM((parts, rows, width), bf16),
            pltpu.VMEM((parts, rows, width), bf16),
            pltpu.VMEM(w_query.shape[1:], bf16),
            pltpu.VMEM(key_value_weight.shape[1:], bf16),
            pltpu.VMEM(w_out.shape[1:], bf16),
            pltpu.VMEM((BLOCK_ROWS, features), bf16),
            pltpu.VMEM((rows, inner), bf16),
            pltpu.VMEM(kv_rows, bf16),
            pltpu.VMEM(kv_rows, bf16),
            pltpu.VMEM((rows, inner), bf16),
        ]
        + [pltpu.VMEM((heads, BLOCK_ROWS, (b + 1) * BLOCK_ROWS), bf16) for b in range(blocks)]
        + [
            pltpu.VMEM((rows, inner), bf16),
            pltpu.VMEM((2, rows, width), bf16),
            pltpu.VMEM((2, rows, width), bf16),
            pltpu.VMEM((rows, width), bf16),
            pltpu.VMEM((rows, width), f32),
            pltpu.VMEM((rows, inner), bf16),
            pltpu.VMEM((rows, HEAD_SIZE), f32),
            pltpu.VMEM((rows, HEAD_SIZE), f32),
            pltpu.VMEM(kv_rows, bf16),
            pltpu.VMEM((rows, 2 * HEAD_SIZE), bf16),
            pltpu.VMEM((4, 8, rows), f32),
            dma((3,)),
            dma((40,)),
            dma((2, 4, chunks)),
            dma((2, 4, chunks)),
            dma((2, blocks)),
            dma((2, blocks)),
            dma((2, blocks)),
            dma((2, blocks)),
            dma((blocks,)),
            dma((blocks,)),
            dma((2,)),
            dma((2,)),
            dma((2, blocks)),
            dma((2, blocks)),
            dma((3,)),
            dma((3,)),
            pltpu.SemaphoreType.REGULAR,
        ],
        compiler_params=pltpu.CompilerParams(
            collective_id=0, has_side_effects=True, vmem_limit_bytes=62 << 20
        ),
        cost_estimate=pl.CostEstimate(
            flops=14 * rows * features * inner, bytes_accessed=60 << 20, transcendentals=heads * rows * rows
        ),
    )(x_handed, cot_handed, w_query, key_value_weight, w_out, norm_gain)


def on_device(x_handed, cot_handed, w_query, key_value_weight, w_out, norm_gain):
    gain_row = norm_gain[0]
    features = gain_row.shape[0]
    me = lax.axis_index("tp")
    (
        x_part, dy_all, normed_all, inv_rms, attended, mixed_far, mixed_near,
        d_queries, d_kv_mine, d_far, d_near, row_dot,
    ) = layer(x_handed, cot_handed, w_query, key_value_weight, w_out, norm_gain)
    far_pairs = [(i, i ^ 2) for i in range(lax.axis_size("tp"))]
    d_far = lax.ppermute(d_far, "tp", far_pairs)
    layer_out = (mixed_near + mixed_far.astype(jnp.float32)).astype(jnp.bfloat16)
    grad_query = dot(normed_all, d_queries, TN).astype(jnp.bfloat16)
    grad_out = dot(attended, dy_all, TN).astype(jnp.bfloat16)
    grad_keyval = dot(normed_all, d_kv_mine, TN).astype(jnp.bfloat16)
    inv_rms = inv_rms[:, :1]
    width = x_part.shape[1]
    mine = me * width
    dy_part = lax.dynamic_slice_in_dim(dy_all, mine, width, 1)
    row_mean = (row_dot[0] / features)[:, None]
    gain_mine = lax.dynamic_slice_in_dim(gain_row, mine, width, 0)
    unit_mine = x_part.astype(jnp.float32) * inv_rms
    d_normed = d_near + d_far.astype(jnp.float32)
    grad_gain = lax.all_gather(jnp.sum(d_normed * unit_mine, axis=0), "tp", tiled=True)
    d_unit = d_normed * gain_mine
    grad_in = (
        dy_part.astype(jnp.float32) + inv_rms * (d_unit - unit_mine * row_mean)
    ).astype(jnp.bfloat16)
    return (
        layer_out[None],
        grad_in[None],
        grad_query[None],
        grad_keyval[None],
        grad_out[None],
        grad_gain[None],
    )


def on_device_any(x_handed, cot_handed, w_query, key_value_weight, w_out, norm_gain):
    x_part = shifted(x_handed, "section", 1)[0]
    dy_part = shifted(cot_handed, "section", -1)[0]
    wq_dev = w_query[0]
    wkv_dev = key_value_weight[0]
    wo_dev = w_out[0]
    gain_row = norm_gain[0]
    heads_per_device = wq_dev.shape[1] // HEAD_SIZE
    score_scale = HEAD_SIZE ** (-0.5)
    x_all = lax.all_gather(x_part, "tp", axis=1, tiled=True)
    sequence_length = x_all.shape[0]
    tok_rows = sequence_length // lax.axis_size("tp")
    row_start = lax.axis_index("tp") * tok_rows
    x_float = x_all.astype(jnp.float32)
    inv_rms = lax.rsqrt(jnp.mean(x_float * x_float, axis=-1, keepdims=True) + 1e-05)
    unit_x = x_float * inv_rms
    normed_all = (unit_x * gain_row).astype(jnp.bfloat16)
    queries = jnp.dot(normed_all, wq_dev, preferred_element_type=jnp.float32).astype(jnp.bfloat16)
    kv_part = jnp.dot(normed_all, wkv_dev, preferred_element_type=jnp.float32).astype(jnp.bfloat16)
    key_value_pairs = lax.all_gather(kv_part, "tp", axis=1, tiled=True)
    key_value_head = lax.axis_index("tp") * heads_per_device // (QUERY_HEADS // KEY_VALUE_HEADS)
    key_rows = lax.dynamic_slice_in_dim(key_value_pairs, key_value_head * HEAD_SIZE, HEAD_SIZE, 1)
    value_rows_full = lax.dynamic_slice_in_dim(
        key_value_pairs, KEY_VALUE_HEADS * HEAD_SIZE + key_value_head * HEAD_SIZE, HEAD_SIZE, 1
    )
    query_heads = queries.reshape(sequence_length, heads_per_device, HEAD_SIZE)
    scores = (
        jnp.einsum("shd,td->hst", query_heads, key_rows, preferred_element_type=jnp.float32)
        * score_scale
    )
    row_ids = lax.broadcasted_iota(jnp.int32, (sequence_length, sequence_length), 0)
    col_ids = lax.broadcasted_iota(jnp.int32, (sequence_length, sequence_length), 1)
    causal = row_ids >= col_ids
    scores = jnp.where(causal[None], scores, jnp.float32(-1e30))
    row_max = jnp.max(scores, axis=-1, keepdims=True)
    shifted_exp = jnp.exp(scores - row_max)
    attn_probs = shifted_exp / jnp.sum(shifted_exp, axis=-1, keepdims=True)
    probs_bf = attn_probs.astype(jnp.bfloat16)
    attended = jnp.einsum(
        "hst,td->shd", probs_bf, value_rows_full, preferred_element_type=jnp.float32
    ).astype(jnp.bfloat16)
    attn_flat = attended.reshape(sequence_length, heads_per_device * HEAD_SIZE)
    out_terms = jnp.dot(attn_flat, wo_dev, preferred_element_type=jnp.float32)
    mixed_part = lax.psum_scatter(
        out_terms.astype(jnp.bfloat16), "tp", scatter_dimension=1, tiled=True
    ).astype(jnp.float32)
    layer_out = (x_part.astype(jnp.float32) + mixed_part).astype(jnp.bfloat16)
    dy_all = lax.all_gather(dy_part, "tp", axis=1, tiled=True)
    grad_out = jnp.einsum(
        "sk,sd->kd", attn_flat, dy_all, preferred_element_type=jnp.float32
    ).astype(jnp.bfloat16)
    d_attended = jnp.einsum("sd,kd->sk", dy_all, wo_dev, preferred_element_type=jnp.float32).astype(
        jnp.bfloat16
    )
    d_att_heads = d_attended.reshape(sequence_length, heads_per_device, HEAD_SIZE)
    d_probs = jnp.einsum(
        "shd,td->hst", d_att_heads, value_rows_full, preferred_element_type=jnp.float32
    )
    row_delta = jnp.einsum(
        "shd,shd->hs", d_att_heads.astype(jnp.float32), attended.astype(jnp.float32)
    )
    d_scores = (attn_probs * (d_probs - row_delta[:, :, None]) * score_scale).astype(jnp.bfloat16)
    d_queries = jnp.einsum("hst,td->shd", d_scores, key_rows, preferred_element_type=jnp.float32)
    d_queries = d_queries.astype(jnp.bfloat16).reshape(
        sequence_length, heads_per_device * HEAD_SIZE
    )
    d_key_rows = jnp.einsum(
        "hst,shd->td", d_scores, query_heads, preferred_element_type=jnp.float32
    )
    value_row_gradient = jnp.einsum(
        "hst,shd->td", probs_bf, d_att_heads, preferred_element_type=jnp.float32
    )
    key_value_contribution = jnp.zeros(
        (sequence_length, 2 * KEY_VALUE_HEADS * HEAD_SIZE), jnp.float32
    )
    key_value_contribution = lax.dynamic_update_slice(
        key_value_contribution, d_key_rows, (jnp.int32(0), key_value_head * HEAD_SIZE)
    )
    key_value_contribution = lax.dynamic_update_slice(
        key_value_contribution,
        value_row_gradient,
        (jnp.int32(0), KEY_VALUE_HEADS * HEAD_SIZE + key_value_head * HEAD_SIZE),
    )
    d_keyvals = lax.psum_scatter(
        key_value_contribution.astype(jnp.bfloat16), "tp", scatter_dimension=1, tiled=True
    )
    grad_query = jnp.einsum(
        "sd,sk->dk", normed_all, d_queries, preferred_element_type=jnp.float32
    ).astype(jnp.bfloat16)
    grad_keyval = jnp.einsum(
        "sd,sk->dk", normed_all, d_keyvals, preferred_element_type=jnp.float32
    ).astype(jnp.bfloat16)
    from_query = jnp.einsum("sk,dk->sd", d_queries, wq_dev, preferred_element_type=jnp.float32)
    from_keyval = jnp.einsum("sk,dk->sd", d_keyvals, wkv_dev, preferred_element_type=jnp.float32)
    d_normed = lax.psum_scatter(
        (from_query + from_keyval).astype(jnp.bfloat16), "tp", scatter_dimension=0, tiled=True
    ).astype(jnp.float32)
    unit_rows = lax.dynamic_slice_in_dim(unit_x, row_start, tok_rows, 0)
    inv_rows = lax.dynamic_slice_in_dim(inv_rms, row_start, tok_rows, 0)
    dy_rows = lax.dynamic_slice_in_dim(dy_all, row_start, tok_rows, 0).astype(jnp.float32)
    gain_local = jnp.sum(d_normed * unit_rows, axis=0)
    grad_gain = lax.psum(gain_local, "tp")
    d_unit = d_normed * gain_row
    d_input = inv_rows * (d_unit - unit_rows * jnp.mean(d_unit * unit_rows, axis=-1, keepdims=True))
    grad_rows = (dy_rows + d_input).astype(jnp.bfloat16)
    grad_in = lax.all_to_all(grad_rows, "tp", split_axis=1, concat_axis=0, tiled=True)
    return (
        layer_out[None],
        grad_in[None],
        grad_query[None],
        grad_keyval[None],
        grad_out[None],
        grad_gain[None],
    )


def solution(mesh):
    return jax.shard_map(
        on_device if mesh.shape["tp"] == KEY_VALUE_HEADS else on_device_any,
        mesh=mesh,
        in_specs=(
            P("section", None, "tp"),
            P("section", None, "tp"),
            P("section", None, "tp"),
            P("section", None, "tp"),
            P("section", "tp", None),
            P("section", None),
        ),
        out_specs=(
            P("section", None, "tp"),
            P("section", None, "tp"),
            P("section", None, "tp"),
            P("section", None, "tp"),
            P("section", "tp", None),
            P("section", None),
        ),
        check_vma=False,
    )
```
